256 devices in a mesh: seq: 128 (over z, y, x), head: 2 (over core).
Axes of the slice: x: 4, y: 4, z: 8, core: 2. Of those that a mesh axis runs over, the one named last changes fastest.
Arguments:
- trunk_query: bfloat16 [65536, 16, 128], P('seq', 'head'), may hold values from -5 to 5
- trunk_key: bfloat16 [65536, 16, 128], P('seq', 'head'), may hold values from -5 to 5
- trunk_value: bfloat16 [65536, 16, 128], P('seq', 'head'), may hold values from -5 to 5
- trunk_wquery: bfloat16 [65536, 16, 128], P('seq', 'head'), may hold values from -5 to 5
- trunk_wkey: bfloat16 [65536, 4, 128], P('seq', 'head'), may hold values from -5 to 5
- trunk_wvalue: bfloat16 [65536, 4, 128], P('seq', 'head'), may hold values from -5 to 5
- branch_query: bfloat16 [131072, 16, 128], P('seq', 'head'), may hold values from -5 to 5
- branch_wquery: bfloat16 [131072, 16, 128], P('seq', 'head'), may hold values from -5 to 5
- branch_wkey: bfloat16 [131072, 4, 128], P('seq', 'head'), may hold values from -5 to 5
- branch_wvalue: bfloat16 [131072, 4, 128], P('seq', 'head'), may hold values from -5 to 5
- level_gain: float32 [16, 11], P('head'), may hold values from 0.1 to 1.9
- fork_block: int32 [128], P('seq'), may hold values from 0 to 3
Outputs:
- trunk_out: bfloat16 [65536, 16, 128], P('seq', 'head')
- branch_out: bfloat16 [131072, 16, 128], P('seq', 'head')
The draws below stay inside these ranges and needn't reach their ends.
All inputs are finite; a program needn't handle non-finite values.
Results may differ from the reference program's by a relative error of at most 0.0045.
The reference program's roundings to bfloat16 on the way count: a program that leaves them out, or rounds other values in their place, can miss the bound.
Values may be sent and summed in bfloat16 or wider, within the bound.
A program may use at most 128 MiB of HBM per device.

```python
import math
from functools import partial
import jax
import jax.numpy as jnp
from jax import lax

DH = 128
BLK = 128
WIN = 512
LEVELS = 11
TOK_DEV = 512
BR_DEV = 1024
NB = 4
H = 16
KVH = 4
TRUNK = 65536
BRANCH = 131072
N_SEQ = 128


def drawn_pair(key, row_count, head_count, kv_groups, head_width, salt):
    base = jax.random.fold_in(key, salt)
    queries = jnp.clip(jax.random.normal(jax.random.fold_in(base, 2), (row_count, head_count, head_width), jnp.float32), -5.0, 5.0)
    key_rows = jnp.clip(jax.random.normal(jax.random.fold_in(base, 3), (row_count, kv_groups, head_width), jnp.float32), -5.0, 5.0)
    return (queries, key_rows)


def draw_trunk_wquery(key, part):
    return drawn_pair(key, TRUNK, H, KVH, DH, 11)[0].astype(jnp.bfloat16)


def draw_trunk_wkey(key, part):
    return drawn_pair(key, TRUNK, H, KVH, DH, 11)[1].astype(jnp.bfloat16)


def draw_branch_wquery(key, part):
    return drawn_pair(key, BRANCH, H, KVH, DH, 23)[0].astype(jnp.bfloat16)


def draw_branch_wkey(key, part):
    return drawn_pair(key, BRANCH, H, KVH, DH, 23)[1].astype(jnp.bfloat16)


def set_ends(values, stream_key, low, largest):
    extent = values.shape
    index_at = [jax.random.randint(jax.random.fold_in(stream_key, axis), (), 0, extent[axis]) for axis in range(len(extent))]
    values = values.at[tuple(index_at)].set(low)
    longest = extent.index(max(extent))
    index_at[longest] = (index_at[longest] + 1) % extent[longest]
    return values.at[tuple(index_at)].set(largest)


def shard_levels(stream_key, shape, pieces, low, high):
    factor_of, own = 1.0, jax.random.fold_in(stream_key, 6)
    for dim, parts in pieces:
        heights = jnp.exp(jax.random.uniform(jax.random.fold_in(own, dim), (parts,), jnp.float32, low / len(pieces), high / len(pieces)))
        factor_of = factor_of * jnp.repeat(heights, shape[dim] // parts).reshape([-1 if axis == dim else 1 for axis in range(len(shape))])
    return factor_of


def centred(own_key, shape, deviation, most, pieces=(), kind=jnp.bfloat16):
    gain = shard_levels(own_key, shape, pieces, -0.22, 0.18) if pieces else 1.0
    drawn = jax.random.normal(own_key, shape, jnp.float32) * deviation * gain
    return jnp.minimum(jnp.maximum(drawn, -most), most).astype(kind)


def setup_inputs(seed: int = 0) -> dict:
    streams_of = jax.random.split(jax.random.key(seed), 13)
    return {
        "trunk_query": centred(streams_of[0], (TRUNK, H, DH), 1.0, 5.0, ((0, 128), (1, 2))),
        "trunk_key": centred(streams_of[1], (TRUNK, H, DH), 1.0, 5.0, ((0, 128), (1, 2))),
        "trunk_value": centred(streams_of[2], (TRUNK, H, DH), 1.0, 5.0, ((0, 128), (1, 2))),
        "trunk_wquery": draw_trunk_wquery(jax.random.fold_in(streams_of[12], 71), 0),
        "trunk_wkey": draw_trunk_wkey(jax.random.fold_in(streams_of[12], 71), 0),
        "trunk_wvalue": centred(streams_of[5], (TRUNK, KVH, DH), 1.0, 5.0, ((0, 128), (1, 2))),
        "branch_query": centred(streams_of[6], (BRANCH, H, DH), 1.0, 5.0, ((0, 128), (1, 2))),
        "branch_wquery": draw_branch_wquery(jax.random.fold_in(streams_of[12], 71), 0),
        "branch_wkey": draw_branch_wkey(jax.random.fold_in(streams_of[12], 71), 0),
        "branch_wvalue": centred(streams_of[9], (BRANCH, KVH, DH), 1.0, 5.0, ((0, 128), (1, 2))),
        "level_gain": jnp.clip(1.0 + 0.18 * jax.random.normal(streams_of[10], (H, LEVELS), jnp.float32), 0.1, 1.9),
        "fork_block": set_ends(jax.random.randint(streams_of[11], (N_SEQ,), 0, NB), jax.random.fold_in(streams_of[11], 1), 0, NB - 1).astype(jnp.int32),
    }


def level_coefficients(level_gain):
    level_index = jnp.arange(LEVELS, dtype=jnp.int32)
    spans = 2.0 ** jnp.maximum(level_index - 1, 0).astype(jnp.float32)
    return level_gain / jnp.sqrt(float(DH * BLK) * spans)[None, :]

def fenwick_step(coefficients, levels, scan_input):
    block_index, queries, key_rows, value_rows = scan_input
    bit_range = jnp.arange(LEVELS - 1, dtype=jnp.int32)
    present = (block_index >> bit_range & 1).astype(jnp.float32)
    attention_probabilities = coefficients[:, 1:] * present[None, :]
    combined = jnp.einsum('hl,lhde->hde', attention_probabilities, levels, precision=lax.Precision.HIGHEST).astype(jnp.bfloat16)
    causal = jnp.arange(BLK)[:, None] >= jnp.arange(BLK)[None, :]
    attention_logits = jnp.einsum('thd,shd->hts', queries.astype(jnp.float32), key_rows.astype(jnp.float32))
    attention_logits = jnp.where(causal[None], attention_logits, 0.0) * coefficients[:, 0][:, None, None]
    inside_weights = lax.optimization_barrier(attention_logits.astype(jnp.bfloat16))
    inside = jnp.einsum('hts,she->the', inside_weights.astype(jnp.float32), value_rows.astype(jnp.float32))
    across = jnp.einsum('thd,hde->the', queries.astype(jnp.float32), combined.astype(jnp.float32))
    block_state = jnp.einsum('thd,the->hde', key_rows.astype(jnp.float32), value_rows.astype(jnp.float32))
    following = block_index + 1
    low_masks = (2 << bit_range) - 1
    below = (block_index & low_masks == low_masks).astype(jnp.float32)
    newest = following & low_masks == 1 << bit_range
    merged = block_state + jnp.einsum('l,lhde->hde', below, levels, precision=lax.Precision.HIGHEST)
    kept = levels * (1.0 - below)[:, None, None, None]
    levels = jnp.where(newest[:, None, None, None], merged[None], kept)
    return (levels, (inside + across, combined))

def window_attend(queries, key_rows, value_rows, offset, first_valid):
    row_count, head_count, head_width = queries.shape
    kv_groups = key_rows.shape[1]
    block_rows = min(512, row_count)
    logit_scale_factor = 1.0 / math.sqrt(head_width)

    def one_block(start_row):
        query_tile_rows = lax.dynamic_slice_in_dim(queries, start_row, block_rows, 0)
        query_tile_rows = query_tile_rows.reshape(block_rows, kv_groups, head_count // kv_groups, head_width)
        key_start = start_row + offset - WIN
        key_tile_rows = lax.dynamic_slice_in_dim(key_rows, key_start, block_rows + WIN, 0)
        value_tile_rows = lax.dynamic_slice_in_dim(value_rows, key_start, block_rows + WIN, 0)
        query_place = start_row + offset + jnp.arange(block_rows, dtype=jnp.int32)
        key_place = key_start + jnp.arange(block_rows + WIN, dtype=jnp.int32)
        allowed = (key_place[None, :] <= query_place[:, None]) & (key_place[None, :] > query_place[:, None] - WIN)
        allowed = allowed & (key_place[None, :] >= first_valid)
        attention_logits = jnp.einsum('nfjx,afx->fjna', query_tile_rows.astype(jnp.float32), key_tile_rows.astype(jnp.float32)) * logit_scale_factor
        attention_logits = jnp.where(allowed[None, None], attention_logits, -1e+30)
        row_max = lax.optimization_barrier(jnp.max(attention_logits, axis=-1, keepdims=True))
        exponent = jnp.exp(attention_logits - row_max)
        row_total = lax.optimization_barrier(jnp.sum(exponent, axis=-1, keepdims=True))
        attention_probabilities = lax.optimization_barrier((exponent / row_total).astype(jnp.bfloat16))
        attended_output = jnp.einsum('yzqa,ayh->qyzh', attention_probabilities.astype(jnp.float32), value_tile_rows.astype(jnp.float32))
        return attended_output.reshape(block_rows, head_count, head_width)
    starts = jnp.arange(row_count // block_rows, dtype=jnp.int32) * block_rows
    return lax.map(one_block, starts).reshape(row_count, head_count, head_width)

def head_norm(output):
    mean_square = lax.optimization_barrier(jnp.mean(output * output, axis=(1, 2), keepdims=True))
    return (output * lax.rsqrt(mean_square + 1e-06)).astype(jnp.bfloat16)

def reference(trunk_query, trunk_key, trunk_value, trunk_wquery, trunk_wkey, trunk_wvalue, branch_query, branch_wquery, branch_wkey, branch_wvalue, level_gain, fork_block):
    coefficients = level_coefficients(level_gain)
    block_total = TRUNK // BLK
    block_shape = (block_total, BLK, H, DH)
    scan_inputs = (jnp.arange(block_total, dtype=jnp.int32), trunk_query.reshape(block_shape), trunk_key.reshape(block_shape), trunk_value.reshape(block_shape))
    empty_levels = jnp.zeros((LEVELS - 1, H, DH, DH), jnp.float32)
    final_levels, (linear_out, mixed) = lax.scan(partial(fenwick_step, coefficients), empty_levels, scan_inputs)
    trunk_linear = linear_out.reshape(TRUNK, H, DH)
    padded_keys = jnp.concatenate([jnp.zeros((WIN, KVH, DH), jnp.bfloat16), trunk_wkey], axis=0)
    padded_values = jnp.concatenate([jnp.zeros((WIN, KVH, DH), jnp.bfloat16), trunk_wvalue], axis=0)
    trunk_window = window_attend(trunk_wquery, padded_keys, padded_values, WIN, WIN)
    trunk_out = head_norm(trunk_linear + trunk_window)
    last_start = (N_SEQ - 1) * NB

    def one_branch(branch_input):
        fork_index, queries, window_queries, window_keys, window_values = branch_input
        end_state = lax.dynamic_index_in_dim(mixed, last_start + fork_index, 0, keepdims=False)
        linear = jnp.einsum('thd,hde->the', queries.astype(jnp.float32), end_state.astype(jnp.float32))
        context_start = ((N_SEQ - 1) * TOK_DEV + fork_index * BLK - WIN).astype(jnp.int32)
        context_keys = lax.dynamic_slice_in_dim(trunk_wkey, context_start, WIN, 0)
        context_values = lax.dynamic_slice_in_dim(trunk_wvalue, context_start, WIN, 0)
        all_keys = jnp.concatenate([context_keys, window_keys], axis=0)
        all_values = jnp.concatenate([context_values, window_values], axis=0)
        window = window_attend(window_queries, all_keys, all_values, WIN, 0)
        return head_norm(linear + window)
    branch_inputs = (fork_block, branch_query.reshape(N_SEQ, BR_DEV, H, DH), branch_wquery.reshape(N_SEQ, BR_DEV, H, DH), branch_wkey.reshape(N_SEQ, BR_DEV, KVH, DH), branch_wvalue.reshape(N_SEQ, BR_DEV, KVH, DH))
    branch_out = lax.map(one_branch, branch_inputs).reshape(BRANCH, H, DH)
    return (trunk_out, branch_out)
```

```python
import functools
import math

import jax
import jax.numpy as jnp
from jax import lax
from jax.experimental import pallas as pl
from jax.experimental.pallas import tpu as pltpu
from jax.sharding import PartitionSpec as P

F32, BF16 = jnp.float32, jnp.bfloat16
MESH = pl.DeviceIdType.MESH
DH = 128
BLK = 128
HD = 8
KV = 2
TB = 4
BB = 8
NX, NY, NZ = 4, 4, 8
NEG = -1e30
EXP2_SCALE = math.log2(math.e) / math.sqrt(DH)
NT = (((1,), (1,)), ((), ()))
NN = (((1,), (0,)), ((), ()))
TN = (((0,), (0,)), ((), ()))


def dot(a, b, dims=NN):
    return lax.dot_general(a, b, dims, preferred_element_type=F32)


def rows_of(start, size):
    return pl.ds(pl.multiple_of(start, size), size)


def split_heads(src, tmp, dst, chunks, heads, dst_start=0):
    size = BLK * heads

    @pl.loop(0, chunks)
    def _(c):
        tmp[pl.ds(0, size), :] = src[rows_of(c * size, size), :].astype(F32)
        for h in range(heads):
            part = tmp[pl.ds(h, BLK, stride=heads), :].astype(BF16)
            dst[h, rows_of(c * BLK + dst_start, BLK), :] = part


def block_states(coef, key, value, tmp, kh, vh, states):
    split_heads(key, tmp, kh, TB, HD)
    split_heads(value, tmp, vh, TB, HD)

    @pl.loop(0, TB)
    def _(b):
        for h in range(HD):
            rows = rows_of(b * BLK, BLK)
            states[b, h * DH : (h + 1) * DH, :] = dot(kh[h, rows, :], vh[h, rows, :], TN)


def local_states(coef, states, local, local_bf, total_bf):
    for h in range(HD):
        rows = slice(h * DH, (h + 1) * DH)
        s0, s1, s2, s3 = (states[b, rows, :] for b in range(TB))
        two = coef[h, 2] * (s0 + s1)
        parts = (coef[h, 1] * s0, two, two + coef[h, 1] * s2)
        for f, part in enumerate(parts):
            local[f, rows, :] = part
            local_bf[f, rows, :] = part.astype(BF16)
        total_bf[rows, :] = ((s0 + s1) + (s2 + s3)).astype(BF16)


def state_kernel(coef, key, value, local, local_bf, total_bf, tmp, kh, vh, states):
    block_states(coef, key, value, tmp, kh, vh, states)
    local_states(coef, states, local, local_bf, total_bf)


def window_block(i, g, qh, kw, vw, out, bad_below, out_start):
    keys = kw[g, pl.ds(pl.multiple_of(i * BLK, BLK), 5 * BLK), :]
    values = vw[g, pl.ds(pl.multiple_of(i * BLK, BLK), 5 * BLK), :]
    rows = rows_of(i * BLK, BLK)
    q = qh[4 * g : 4 * g + 4, rows, :].reshape(4 * BLK, DH)
    s = dot(q, keys, NT)
    row = lax.broadcasted_iota(jnp.int32, (4 * BLK, BLK), 0) & (BLK - 1)
    col = lax.broadcasted_iota(jnp.int32, (4 * BLK, BLK), 1)
    own = col <= row
    tiles = [s[:, j * BLK : (j + 1) * BLK] for j in range(5)]
    if bad_below is not None:
        for j in range(4):
            tiles[j] = jnp.where(i + j < bad_below, NEG, tiles[j])
    tiles = [jnp.where(own, tiles[4], tiles[0])] + tiles[1:4]
    top = jnp.maximum(jnp.maximum(tiles[0], tiles[1]), jnp.maximum(tiles[2], tiles[3]))
    top = jnp.max(top, axis=-1, keepdims=True) * EXP2_SCALE
    ex = [jnp.exp2(t * EXP2_SCALE - top) for t in tiles]
    total = jnp.sum((ex[0] + ex[1]) + (ex[2] + ex[3]), axis=-1, keepdims=True)
    inv = 1.0 / total
    edge = ex[0] * inv
    pieces = [jnp.where(own, 0.0, edge).astype(BF16)]
    pieces += [(e * inv).astype(BF16) for e in ex[1:]]
    pieces += [jnp.where(own, edge, 0.0).astype(BF16)]
    o = dot(jnp.concatenate(pieces, axis=1), values)
    out[4 * g : 4 * g + 4, rows_of(out_start + i * BLK, BLK), :] = o.reshape(4, BLK, DH)


def trunk_linear_block(b, coef, qh, kh, vh, local, cross, out):
    rows = rows_of(b * BLK, BLK)
    row = lax.broadcasted_iota(jnp.int32, (BLK, BLK), 0)
    col = lax.broadcasted_iota(jnp.int32, (BLK, BLK), 1)
    for h in range(HD):
        hr = slice(h * DH, (h + 1) * DH)
        q = qh[h, rows, :]
        s = dot(q, kh[h, rows, :], NT)
        w = jnp.where(col <= row, s * coef[h, 0], 0.0).astype(BF16)
        loc = jnp.where(b == 0, 0.0, local[jnp.maximum(b - 1, 0), hr, :])
        combined = (cross[hr, :].astype(F32) + loc).astype(BF16)
        out[h, rows, :] = out[h, rows, :] + (dot(w, vh[h, rows, :]) + dot(q, combined))


def square_sums(out, chunk, ss):
    acc = None
    for h in range(HD):
        o = out[h, rows_of(chunk * BLK, BLK), :]
        acc = o * o if acc is None else acc + o * o
    ss[pl.ds(chunk, 1), :] = jnp.sum(acc.T, axis=0, keepdims=True)


def attend_kernel(coef, fork, tq, tk, tv, twq, twk, twv, kprev, vprev, bq, bwq, bwk, bwv,
                  kctx, vctx, local, cross, ecross, lbc, out, ss,
                  tmp, qh, kh, vh, wqh, bqh, kt, vt, kb, vb, end):
    s = lax.axis_index("seq")
    split_heads(tq, tmp, qh, TB, HD)
    split_heads(tk, tmp, kh, TB, HD)
    split_heads(tv, tmp, vh, TB, HD)
    split_heads(twq, tmp, wqh, TB, HD)
    split_heads(bwq, tmp, wqh, BB, HD, TB * BLK)
    split_heads(bq, tmp, bqh, BB, HD)
    split_heads(kprev, tmp, kt, TB, KV)
    split_heads(vprev, tmp, vt, TB, KV)
    split_heads(twk, tmp, kt, TB, KV, TB * BLK)
    split_heads(twv, tmp, vt, TB, KV, TB * BLK)
    split_heads(bwk, tmp, kb, BB, KV, TB * BLK)
    split_heads(bwv, tmp, vb, BB, KV, TB * BLK)
    f = fork[0]
    for j in range(TB):
        for src, dst in ((kctx, kb), (vctx, vb)):
            tmp[0 : KV * BLK, :] = src[f + j].astype(F32)
            for g in range(KV):
                dst[g, j * BLK : (j + 1) * BLK, :] = tmp[pl.ds(g, BLK, stride=KV), :].astype(BF16)
    bad = jnp.where(s == 0, TB, 0)
    tqr = wqh.at[:, pl.ds(0, TB * BLK), :]
    bqr = wqh.at[:, pl.ds(TB * BLK, BB * BLK), :]

    @pl.loop(0, TB)
    def _(i):
        for g in range(KV):
            window_block(i, g, tqr, kt, vt, out, bad, 0)

    @pl.loop(0, BB)
    def _(i):
        for g in range(KV):
            window_block(i, g, bqr, kb, vb, out, None, TB * BLK)

    @pl.loop(0, TB)
    def _(b):
        trunk_linear_block(b, coef, qh, kh, vh, local, cross, out)

    branch_linear(f, bqh, ecross, lbc, end, out)

    @pl.loop(0, TB + BB)
    def _(c):
        square_sums(out, c, ss)


def branch_linear(f, bqh, ecross, lbc, end, out):
    loc = jnp.where(f == 0, 0.0, lbc[jnp.maximum(f - 1, 0)].astype(F32))
    end[...] = (ecross[...].astype(F32) + loc).astype(BF16)

    @pl.loop(0, HD)
    def _(h):
        er = end[rows_of(h * DH, DH), :]
        for c in range(2):
            src = slice(c * 512, (c + 1) * 512)
            dst = slice(TB * BLK + c * 512, TB * BLK + (c + 1) * 512)
            out[h, dst, :] = out[h, dst, :] + dot(bqh[h, src, :], er)


def scale_kernel(out, ss, trunk_out, branch_out, tmp):

    def chunk(c, dst, dst_chunk):
        r = lax.rsqrt(ss[pl.ds(c, 1), :] / (2 * HD * DH) + 1e-6)
        scale = jnp.broadcast_to(r, (BLK, BLK)).T
        for h in range(HD):
            tmp[pl.ds(h, BLK, stride=HD), :] = out[h, rows_of(c * BLK, BLK), :] * scale
        dst[rows_of(dst_chunk * BLK * HD, BLK * HD), :] = tmp[...].astype(BF16)

    @pl.loop(0, TB)
    def _(c):
        chunk(c, trunk_out, c)

    @pl.loop(0, BB)
    def _(c):
        chunk(c + TB, branch_out, c)


VM = pl.BlockSpec(memory_space=pltpu.VMEM)
SM = pl.BlockSpec(memory_space=pltpu.SMEM)
VMEM_LIMIT = 60 * 1024 * 1024


def sds(shape, dtype):
    return jax.ShapeDtypeStruct(shape, dtype)


def neighbours(x, y, z):
    group = []
    for d in range(1, NX):
        group.append((z * 16 + y * 4 + lax.rem(x + d, NX)))
    for d in range(1, NY):
        group.append((z * 16 + lax.rem(y + d, NY) * 4 + x))
    for d in range(1, NZ):
        group.append((lax.rem(z + d, NZ) * 16 + y * 4 + x))
    return group


def comm_kernel(coef, total, local_bf, wk, wv,
                cross, ecross, lbc, kvbc, kprev, vprev,
                xin, yin, zin, exin, ezin, yret, ysend, xsend, ry, rs,
                px_s, px_r, nb_s, nb_r, b1_s, b1_r, b2_s, b2_r, b3_s, b3_r, b4_s, b4_r,
                b5_s, b5_r, y_s, y_r, ey_s, ey_r, z_s, z_r, ez_s, ez_r, yr_s, yr_r, xr_s, xr_r):
    s = lax.axis_index("seq")
    head = lax.axis_index("head")
    n = NX * NY * NZ
    x, y, z = lax.rem(s, NX), lax.rem(s // NX, NY), s // (NX * NY)
    barrier = pltpu.get_barrier_semaphore()
    group = neighbours(x, y, z)
    for other in group:
        pl.semaphore_signal(barrier, inc=1, device_id=(other, head), device_id_type=MESH)
    for other in (lax.rem(s + 1, n), lax.rem(s + n - 1, n)):
        pl.semaphore_signal(barrier, inc=1, device_id=(other, head), device_id_type=MESH)
    pl.semaphore_wait(barrier, len(group) + 2)
    has_prev, has_next = s > 0, s < n - 1

    def send(src, dst, ssem, rsem, to):
        return pltpu.make_async_remote_copy(
            src_ref=src, dst_ref=dst, send_sem=ssem, recv_sem=rsem,
            device_id=(to, head), device_id_type=MESH)

    def x_dev(v):
        return z * 16 + y * 4 + v

    def y_dev(v):
        return z * 16 + v * 4 + x

    def z_dev(v):
        return v * 16 + y * 4 + x

    wrap = lax.rem
    xr = lambda v: rows_of(v * 256, 256)

    x_copies = []
    for d in range(1, NX):
        to = wrap(x + d, NX)
        c = send(total.at[xr(to), :], xin.at[x], px_s.at[d - 1], px_r.at[d - 1], x_dev(to))
        c.start()
        x_copies.append(c)

    nb = [send(a, b, nb_s.at[k], nb_r.at[k], jnp.minimum(s + 1, n - 1))
          for k, (a, b) in enumerate(((wk, kprev), (wv, vprev)))]

    @pl.when(has_next)
    def _():
        for c in nb:
            c.start()

    last, before = s == n - 1, s == n - 2
    row_y = (y == NY - 1) & (z == NZ - 1)

    def b1(d, sem_base):
        to = wrap(x + d, NX)
        kr = rows_of(to * 64, 64)
        a = send(local_bf.at[:, xr(to), :], lbc.at[:, xr(to), :], b1_s.at[d - 1, 0], b1_r.at[0], x_dev(to))
        out = []
        for k, src in enumerate((wk, wv)):
            out.append((
                send(src.at[pl.ds(0, 3), kr, :], kvbc.at[k, pl.ds(4, 3), kr, :], b1_s.at[d - 1, 1 + k], b1_r.at[1 + k], x_dev(to)),
                send(src.at[:, kr, :], kvbc.at[k, pl.ds(0, 4), kr, :], b1_s.at[d - 1, 1 + k], b1_r.at[3 + k], x_dev(to))))
        return a, out

    stage1 = [b1(d, 0) for d in range(1, NX)]

    @pl.when(last)
    def _():
        for a, kv in stage1:
            a.start()
            for c7, _ in kv:
                c7.start()
        mine = xr(x)
        lbc[:, mine, :] = local_bf[:, mine, :]
        kr = rows_of(x * 64, 64)
        kvbc[0, 4:7, kr, :] = wk[0:3, kr, :]
        kvbc[1, 4:7, kr, :] = wv[0:3, kr, :]

    @pl.when(before)
    def _():
        for a, kv in stage1:
            for _, c6 in kv:
                c6.start()
        kr = rows_of(x * 64, 64)
        kvbc[0, 0:4, kr, :] = wk[:, kr, :]
        kvbc[1, 0:4, kr, :] = wv[:, kr, :]

    xin[x] = total[xr(x), :]
    for c in x_copies:
        c.wait()
    h0 = 2 * x

    def fenwick4(parts, lo, hi):
        two = hi * (parts[0] + parts[1])
        return [None, lo * parts[0], two, two + lo * parts[2]]

    tx = []
    for hh in range(2):
        hr = slice(hh * DH, (hh + 1) * DH)
        parts = [xin[v, hr, :].astype(F32) for v in range(NX)]
        rs[hr, :] = (parts[0] + parts[1]) + (parts[2] + parts[3])

    y_copies = []
    for d in range(1, NY):
        to = wrap(y + d, NY)
        c = send(rs.at[rows_of(to * 64, 64), :], yin.at[y], y_s.at[d - 1], y_r.at[d - 1], y_dev(to))
        c.start()
        y_copies.append(c)
    yin[y] = rs[rows_of(y * 64, 64), :]

    for hh in range(2):
        hr = slice(hh * DH, (hh + 1) * DH)
        parts = [xin[v, hr, :].astype(F32) for v in range(NX)]
        ry[hr, :] = fenwick4(parts, coef[h0 + hh, 3], coef[h0 + hh, 4])[3]
    ey = []
    for d in range(1, NY):
        to = wrap(y + d, NY)
        ey.append(send(ry.at[rows_of(to * 64, 64), :], exin, ey_s.at[d - 1], ey_r, y_dev(to)))

    @pl.when(row_y)
    def _():
        for c in ey:
            c.start()
        exin[...] = ry[rows_of(y * 64, 64), :]

    def b2(d):
        to = wrap(y + d, NY)
        lr = rows_of(x * 256 + to * 64, 64)
        kr = rows_of(x * 64 + to * 16, 16)
        return [send(lbc.at[:, lr, :], lbc.at[:, lr, :], b2_s.at[d - 1, 0], b2_r.at[0], y_dev(to)),
                send(kvbc.at[:, :, kr, :], kvbc.at[:, :, kr, :], b2_s.at[d - 1, 1], b2_r.at[1], y_dev(to))]

    stage2 = [b2(d) for d in range(1, NY)]

    @pl.when(row_y)
    def _():
        @pl.when(x != NX - 1)
        def _():
            a, kv = stage1[0]
            a.wait_recv()
            kv[0][0].wait_recv()
            kv[1][0].wait_recv()

        @pl.when(x != NX - 2)
        def _():
            a, kv = stage1[0]
            kv[0][1].wait_recv()
            kv[1][1].wait_recv()

        for pair in stage2:
            for c in pair:
                c.start()

    for c in y_copies:
        c.wait()
    hy = 2 * x + y // 2
    yparts = [yin[v] for v in range(NY)]
    cy = fenwick4(yparts, coef[hy, 5], coef[hy, 6])
    zin[z] = (yparts[0] + yparts[1]) + (yparts[2] + yparts[3])
    z_copies = []
    for d in range(1, NZ):
        to = wrap(z + d, NZ)
        c = send(zin.at[z], zin.at[z], z_s.at[d - 1], z_r.at[d - 1], z_dev(to))
        c.start()
        z_copies.append(c)

    lr1 = rows_of(x * 256 + y * 64, 64)
    kr1 = rows_of(x * 64 + y * 16, 16)
    ez, stage3 = [], []
    for d in range(1, NZ):
        to = wrap(z + d, NZ)
        ez.append(send(ezin, ezin, ez_s.at[d - 1], ez_r, z_dev(to)))
        stage3.append([
            send(lbc.at[:, lr1, :], lbc.at[:, lr1, :], b3_s.at[d - 1, 0], b3_r.at[0], z_dev(to)),
            send(kvbc.at[:, :, kr1, :], kvbc.at[:, :, kr1, :], b3_s.at[d - 1, 1], b3_r.at[1], z_dev(to))])
    last_plane = z == NZ - 1

    @pl.when(last_plane)
    def _():
        @pl.when(y != NY - 1)
        def _():
            ey[0].wait_recv()
            for c in stage2[0]:
                c.wait_recv()

        ezin[...] = exin[...] + cy[3]
        for c in ez:
            c.start()
        for pair in stage3:
            for c in pair:
                c.start()

    @pl.when(jnp.logical_not(last_plane))
    def _():
        ez[0].wait_recv()

    for c in z_copies:
        c.wait()
    zp = [zin[v] for v in range(NZ)]
    c7, c8, c9 = coef[hy, 7], coef[hy, 8], coef[hy, 9]
    z0, z1, z2 = z & 1, (z >> 1) & 1, (z >> 2) & 1
    lower = z2 == 0
    half = (zp[0] + zp[1]) + (zp[2] + zp[3])
    low_pair = zp[0] + zp[1]
    high_pair = zp[4] + zp[5]
    cz = jnp.where(z2 == 1, c9 * half, 0.0)
    cz = cz + jnp.where(z1 == 1, c8 * jnp.where(lower, low_pair, high_pair), 0.0)
    one = zin[z & 6]
    cz = cz + jnp.where(z0 == 1, c7 * one, 0.0)
    cz_last = c9 * half + c8 * high_pair + c7 * zp[6]
    for v in range(NY):
        ysend[v, 0] = cz if cy[v] is None else cz + cy[v]
        ysend[v, 1] = ezin[...] + cz_last

    yr_copies = []
    for d in range(1, NY):
        to = wrap(y + d, NY)
        c = send(ysend.at[to], yret.at[y], yr_s.at[d - 1], yr_r.at[d - 1], y_dev(to))
        c.start()
        yr_copies.append(c)
    yret[y] = ysend[y]
    stage4 = []
    for d in range(1, NY):
        to = wrap(y + d, NY)
        stage4.append([
            send(lbc.at[:, lr1, :], lbc.at[:, lr1, :], b4_s.at[d - 1, 0], b4_r.at[d - 1, 0], y_dev(to)),
            send(kvbc.at[:, :, kr1, :], kvbc.at[:, :, kr1, :], b4_s.at[d - 1, 1], b4_r.at[d - 1, 1], y_dev(to))])

    @pl.when(jnp.logical_not(last_plane))
    def _():
        for c in stage3[0]:
            c.wait_recv()

    def stage4_each(act):
        for d in range(1, NY):
            @pl.when(jnp.logical_not(last_plane & (wrap(y + d, NY) == NY - 1)))
            def _():
                for c in stage4[d - 1]:
                    act(c)

    stage4_each(lambda c: c.start())
    for c in yr_copies:
        c.wait()

    for v in range(NX):
        for yy in range(NY):
            hh = yy // 2
            hr = slice(yy * 64, (yy + 1) * 64)
            parts = [xin[u, hr, :].astype(F32) for u in range(NX)]
            cx = fenwick4(parts, coef[h0 + hh, 3], coef[h0 + hh, 4])[v]
            r = yret[yy, 0]
            xsend[v, hr, :] = (r if cx is None else r + cx).astype(BF16)
            if v == 0:
                xsend[NX, hr, :] = yret[yy, 1].astype(BF16)
    xr_copies = []
    mine = xr(x)
    for d in range(1, NX):
        to = wrap(x + d, NX)
        for k, (src, dst) in enumerate(((xsend.at[to], cross), (xsend.at[NX], ecross))):
            c = send(src, dst.at[mine, :], xr_s.at[d - 1, k], xr_r.at[d - 1, k], x_dev(to))
            c.start()
            xr_copies.append(c)
    cross[mine, :] = xsend[x]
    ecross[mine, :] = xsend[NX]
    stage4_each(lambda c: c.wait_send())

    @pl.when(jnp.logical_not(row_y))
    def _():
        for pair in stage4:
            for c in pair:
                c.wait_recv()

    kr4 = rows_of(x * 64, 64)
    stage5 = []
    for d in range(1, NX):
        to = wrap(x + d, NX)
        stage5.append(send(lbc.at[:, mine, :], lbc.at[:, mine, :], b5_s.at[d - 1, 0], b5_r.at[d - 1, 0], x_dev(to)))
        stage5.append(send(kvbc.at[:, :, kr4, :], kvbc.at[:, :, kr4, :], b5_s.at[d - 1, 1], b5_r.at[d - 1, 1], x_dev(to)))
    for c in stage5:
        c.start()
    for c in xr_copies:
        c.wait()
    for c in stage5:
        c.wait()

    @pl.when(has_next)
    def _():
        for c in nb:
            c.wait_send()

    @pl.when(has_prev)
    def _():
        for c in nb:
            c.wait_recv()

    @pl.when(jnp.logical_not(has_prev))
    def _():
        kprev[...] = jnp.zeros_like(kprev)
        vprev[...] = jnp.zeros_like(vprev)

    @pl.when(last)
    def _():
        for a, kv in stage1:
            a.wait_send()
            for c7, _ in kv:
                c7.wait_send()

    @pl.when(before)
    def _():
        for a, kv in stage1:
            for _, c6 in kv:
                c6.wait_send()

    @pl.when(row_y)
    def _():
        for c in ey:
            c.wait_send()
        for pair in stage2:
            for c in pair:
                c.wait_send()

    @pl.when(last_plane)
    def _():
        for c in ez:
            c.wait_send()
        for pair in stage3:
            for c in pair:
                c.wait_send()


def shards(tq, tk, tv, twq, twk, twv, bq, bwq, bwk, bwv, gain, fork):
    flat = lambda a: a.reshape(-1, DH)
    tq, tk, tv, twq, bq, bwq = map(flat, (tq, tk, tv, twq, bq, bwq))
    twk, twv, bwk, bwv = map(flat, (twk, twv, bwk, bwv))
    scale = [1.0 / math.sqrt(DH * BLK * 2 ** max(l - 1, 0)) for l in range(gain.shape[1])]
    coef = gain * jnp.asarray(scale, F32)[None, :]
    params = functools.partial(pltpu.CompilerParams, vmem_limit_bytes=VMEM_LIMIT)
    R = HD * DH
    local, local_bf, total = pl.pallas_call(
        state_kernel, name="states",
        out_shape=(sds((3, R, DH), F32), sds((3, R, DH), BF16), sds((R, DH), BF16)),
        in_specs=[SM, VM, VM], out_specs=(VM, VM, VM),
        scratch_shapes=[pltpu.VMEM((BLK * HD, DH), F32), pltpu.VMEM((HD, TB * BLK, DH), BF16),
                        pltpu.VMEM((HD, TB * BLK, DH), BF16), pltpu.VMEM((TB, R, DH), F32)],
        compiler_params=params(),
    )(coef, tk, tv)
    D = pltpu.SemaphoreType.DMA
    cross, ecross, lbc, kvbc, kprev, vprev = pl.pallas_call(
        comm_kernel, name="exchange",
        out_shape=(sds((R, DH), BF16), sds((R, DH), BF16), sds((3, R, DH), BF16),
                   sds((2, 7, 256, DH), BF16), sds((4, 256, DH), BF16), sds((4, 256, DH), BF16)),
        in_specs=[SM] + [VM] * 4, out_specs=(VM,) * 6,
        scratch_shapes=[
            pltpu.VMEM((NX, 256, DH), BF16), pltpu.VMEM((NY, 64, DH), F32), pltpu.VMEM((NZ, 64, DH), F32),
            pltpu.VMEM((64, DH), F32), pltpu.VMEM((64, DH), F32), pltpu.VMEM((NY, 2, 64, DH), F32),
            pltpu.VMEM((NY, 2, 64, DH), F32), pltpu.VMEM((NX + 1, 256, DH), BF16),
            pltpu.VMEM((256, DH), F32), pltpu.VMEM((256, DH), F32),
            D((3,)), D((3,)), D((2,)), D((2,)), D((3, 3)), D((5,)), D((3, 2)), D((2,)), D((7, 2)), D((2,)),
            D((3, 2)), D((3, 2)), D((3, 2)), D((3, 2)), D((3,)), D((3,)), D((3,)), D, D((7,)), D((7,)),
            D((7,)), D, D((3,)), D((3,)), D((3, 2)), D((3, 2))],
        compiler_params=params(collective_id=0, has_side_effects=True),
    )(coef, total, local_bf, twk.reshape(4, 256, DH), twv.reshape(4, 256, DH))
    T = (TB + BB) * BLK
    out, ss = pl.pallas_call(
        attend_kernel, name="attend",
        out_shape=(sds((HD, T, DH), F32), sds((TB + BB, DH), F32)),
        in_specs=[SM, SM] + [VM] * 18, out_specs=(VM, VM),
        scratch_shapes=[pltpu.VMEM((BLK * HD, DH), F32)]
        + [pltpu.VMEM((HD, TB * BLK, DH), BF16)] * 3
        + [pltpu.VMEM((HD, T, DH), BF16), pltpu.VMEM((HD, BB * BLK, DH), BF16)]
        + [pltpu.VMEM((KV, 2 * TB * BLK, DH), BF16)] * 2
        + [pltpu.VMEM((KV, (TB + BB) * BLK, DH), BF16)] * 2
        + [pltpu.VMEM((R, DH), BF16)],
        compiler_params=params(),
    )(coef, fork, tq, tk, tv, twq, twk, twv, flat(kprev), flat(vprev), bq, bwq, bwk, bwv,
      kvbc[0], kvbc[1], local, cross, ecross, lbc)
    ss = lax.psum(ss, "head")
    trunk_out, branch_out = pl.pallas_call(
        scale_kernel, name="scale",
        out_shape=(sds((TB * BLK * HD, DH), BF16), sds((BB * BLK * HD, DH), BF16)),
        in_specs=[VM, VM], out_specs=(VM, VM),
        scratch_shapes=[pltpu.VMEM((BLK * HD, DH), F32)],
        compiler_params=params(),
    )(out, ss)
    return trunk_out.reshape(TB * BLK, HD, DH), branch_out.reshape(BB * BLK, HD, DH)


def solution(mesh):
    spec = P("seq", "head", None)
    return jax.shard_map(
        shards, mesh=mesh, in_specs=(spec,) * 10 + (P("head", None), P("seq")),
        out_specs=(spec, spec), check_vma=False)
```

```python
import functools
import math

import jax
import jax.numpy as jnp
from jax import lax
from jax.experimental import pallas as pl
from jax.experimental.pallas import tpu as pltpu
from jax.sharding import PartitionSpec as P

F32, BF16 = jnp.float32, jnp.bfloat16
MESH = pl.DeviceIdType.MESH
DH = 128
BLK = 128
HD = 8
KV = 2
TB = 4
BB = 8
NX, NY, NZ = 4, 4, 8
NEG = -1e30
EXP2_SCALE = math.log2(math.e) / math.sqrt(DH)
NT = (((1,), (1,)), ((), ()))
NN = (((1,), (0,)), ((), ()))
TN = (((0,), (0,)), ((), ()))


def dot(a, b, dims=NN):
    return lax.dot_general(a, b, dims, preferred_element_type=F32)


def rows_of(start, size):
    return pl.ds(pl.multiple_of(start, size), size)


def split_heads(src, tmp, dst, chunks, heads, dst_start=0):
    size = BLK * heads

    @pl.loop(0, chunks)
    def _(c):
        tmp[pl.ds(0, size), :] = src[rows_of(c * size, size), :].astype(F32)
        for h in range(heads):
            part = tmp[pl.ds(h, BLK, stride=heads), :].astype(BF16)
            dst[h, rows_of(c * BLK + dst_start, BLK), :] = part


def level_weight(gain, h, level):
    return gain[h, level] * (1.0 / math.sqrt(DH * BLK * 2 ** max(level - 1, 0)))


def block_states(kh, vh, states):
    @pl.loop(0, TB)
    def _(b):
        rows = rows_of(b * BLK, BLK)
        for h in range(HD):
            states[b, h * DH : (h + 1) * DH, :] = dot(kh[h, rows, :], vh[h, rows, :], TN)


def local_states(coef, states, local, local_bf, total_bf):
    for h in range(HD):
        rows = slice(h * DH, (h + 1) * DH)
        c1, c2 = coef(h, 1), coef(h, 2)
        s0, s1, s2, s3 = (states[b, rows, :] for b in range(TB))
        two = c2 * (s0 + s1)
        parts = (c1 * s0, two, two + c1 * s2)
        for f, part in enumerate(parts):
            local[f, rows, :] = part
            local_bf[f, rows, :] = part.astype(BF16)
        total_bf[rows, :] = ((s0 + s1) + (s2 + s3)).astype(BF16)


def window_block(i, g, qh, kw, vw, out, bad_below, out_start):
    keys = kw[g, pl.ds(pl.multiple_of(i * BLK, BLK), 5 * BLK), :]
    values = vw[g, pl.ds(pl.multiple_of(i * BLK, BLK), 5 * BLK), :]
    rows = rows_of(i * BLK, BLK)
    q = qh[4 * g : 4 * g + 4, rows, :].reshape(4 * BLK, DH)
    s = dot(q, keys, NT)
    row = lax.broadcasted_iota(jnp.int32, (4 * BLK, BLK), 0) & (BLK - 1)
    col = lax.broadcasted_iota(jnp.int32, (4 * BLK, BLK), 1)
    own = col <= row
    tiles = [s[:, j * BLK : (j + 1) * BLK] for j in range(5)]
    if bad_below is not None:
        for j in range(4):
            tiles[j] = jnp.where(i + j < bad_below, NEG, tiles[j])
    tiles = [jnp.where(own, tiles[4], tiles[0])] + tiles[1:4]
    top = jnp.maximum(jnp.maximum(tiles[0], tiles[1]), jnp.maximum(tiles[2], tiles[3]))
    top = jnp.max(top, axis=-1, keepdims=True) * EXP2_SCALE
    ex = [jnp.exp2(t * EXP2_SCALE - top) for t in tiles]
    total = jnp.sum((ex[0] + ex[1]) + (ex[2] + ex[3]), axis=-1, keepdims=True)
    inv = 1.0 / total
    edge = ex[0] * inv
    pieces = [jnp.where(own, 0.0, edge).astype(BF16)]
    pieces += [(e * inv).astype(BF16) for e in ex[1:]]
    pieces += [jnp.where(own, edge, 0.0).astype(BF16)]
    o = dot(jnp.concatenate(pieces, axis=1), values)
    out[4 * g : 4 * g + 4, rows_of(out_start + i * BLK, BLK), :] = o.reshape(4, BLK, DH)


def trunk_linear_block(b, coef, qh, kh, vh, local, cross, out):
    rows = rows_of(b * BLK, BLK)
    row = lax.broadcasted_iota(jnp.int32, (BLK, BLK), 0)
    col = lax.broadcasted_iota(jnp.int32, (BLK, BLK), 1)
    for h in range(HD):
        hr = slice(h * DH, (h + 1) * DH)
        q = qh[h, rows, :]
        s = dot(q, kh[h, rows, :], NT)
        w = jnp.where(col <= row, s * coef(h, 0), 0.0).astype(BF16)
        loc = jnp.where(b == 0, 0.0, local[jnp.maximum(b - 1, 0), hr, :])
        combined = (cross[hr, :].astype(F32) + loc).astype(BF16)
        out[h, rows, :] = out[h, rows, :] + (dot(w, vh[h, rows, :]) + dot(q, combined))


def square_sums(out, chunk, ss):
    acc = None
    for h in range(HD):
        o = out[h, rows_of(chunk * BLK, BLK), :]
        acc = o * o if acc is None else acc + o * o
    ss[pl.ds(chunk, 1), :] = jnp.sum(acc.T, axis=0, keepdims=True)


def branch_linear(bqh, end, out):
    @pl.loop(0, HD)
    def _(h):
        er = end[rows_of(h * DH, DH), :]
        for c in range(2):
            src = slice(c * 512, (c + 1) * 512)
            dst = slice(TB * BLK + c * 512, TB * BLK + (c + 1) * 512)
            out[h, dst, :] = out[h, dst, :] + dot(bqh[h, src, :], er)


def scale_chunk(c, out, ss_own, ss_other, tmp, obuf):
    total = ss_own[pl.ds(c, 1), :] + ss_other[pl.ds(c, 1), :]
    r = lax.rsqrt(total / (2 * HD * DH) + 1e-6)
    scale = jnp.broadcast_to(r, (BLK, BLK)).T
    for h in range(HD):
        tmp[pl.ds(h, BLK, stride=HD), :] = out[h, rows_of(c * BLK, BLK), :] * scale
    obuf[rows_of(c * BLK * HD, BLK * HD), :] = tmp[...].astype(BF16)


def fenwick4(parts, lo, hi):
    two = hi * (parts[0] + parts[1])
    return [None, lo * parts[0], two, two + lo * parts[2]]


def pick(f, options):
    chosen = options[0]
    for k in range(1, len(options)):
        chosen = jnp.where(f == k, options[k], chosen)
    return chosen


INPUTS = ("tk", "tv", "twk", "twv", "bwk", "bwv", "bwq", "twq", "tq", "bq")


class Refs:
    pass


def fused_kernel(names, *refs):
    r = Refs()
    for name, ref in zip(names, refs):
        setattr(r, name, ref)
    coef = functools.partial(level_weight, r.gain)
    s = lax.axis_index("seq")
    head = lax.axis_index("head")
    n = NX * NY * NZ
    x, y, z = lax.rem(s, NX), lax.rem(s // NX, NY), s // (NX * NY)
    wrap = lax.rem

    loads = {}
    for k, name in enumerate(INPUTS):
        loads[name] = pltpu.make_async_copy(getattr(r, name), getattr(r, "v_" + name), r.load_sem.at[k])
        loads[name].start()

    barrier = pltpu.get_barrier_semaphore()
    peers = [(v, head) for v in neighbours(x, y, z)]
    peers += [(wrap(s + 1, n), head), (wrap(s + n - 1, n), head), (s, 1 - head)]
    for peer in peers:
        pl.semaphore_signal(barrier, inc=1, device_id=peer, device_id_type=MESH)
    r.fk[NX + NY] = jnp.full((8, DH), r.fork[0], jnp.int32).astype(F32)
    pl.semaphore_wait(barrier, len(peers))

    def send(src, dst, ssem, rsem, to):
        if not isinstance(to, tuple):
            to = (to, head)
        return pltpu.make_async_remote_copy(
            src_ref=src, dst_ref=dst, send_sem=ssem, recv_sem=rsem, device_id=to, device_id_type=MESH)

    def x_dev(v):
        return z * 16 + y * 4 + v

    def y_dev(v):
        return z * 16 + v * 4 + x

    def z_dev(v):
        return v * 16 + y * 4 + x

    xs = [wrap(x + d, NX) for d in range(1, NX)]
    ys = [wrap(y + d, NY) for d in range(1, NY)]
    zs = [wrap(z + d, NZ) for d in range(1, NZ)]
    has_prev, has_next = s > 0, s < n - 1
    last, before = s == n - 1, s == n - 2
    last_plane = z == NZ - 1
    row_y = (y == NY - 1) & last_plane
    mine_x = rows_of(x * 256, 256)
    q64 = lambda v: rows_of(v * 64, 64)
    q16 = rows_of(y * 64 + x * 16, 16)

    def start(copies):
        for c in copies:
            c.start()

    def wait_send(copies):
        for c in copies:
            c.wait_send()

    def wait_recv(copies):
        for c in copies:
            c.wait_recv()

    fork_copies = [send(r.fk.at[NX + NY], r.fk.at[x], r.fk_s.at[d], r.fk_r.at[d], x_dev(to)) for d, to in enumerate(xs)]
    fork_copies += [send(r.fk.at[NX + NY], r.fk.at[NX + y], r.fk_s.at[3 + d], r.fk_r.at[3 + d], y_dev(to))
                    for d, to in enumerate(ys)]
    start(fork_copies)

    nxt = jnp.minimum(s + 1, n - 1)
    nb = [send(a, b, r.nb_s.at[k], r.nb_r.at[k], nxt) for k, (a, b) in enumerate(((r.twk, r.kprev), (r.twv, r.vprev)))]
    k1_last, k1_before = [], []
    for d, to in enumerate(ys):
        for k, src in enumerate((r.twk, r.twv)):
            k1_last.append(send(src.at[pl.ds(0, 3), q64(to), :], r.k1.at[k, pl.ds(0, 3)], r.k1_s.at[d, k], r.k1_r.at[k], y_dev(to)))
            k1_before.append(send(src.at[:, q64(to), :], r.k1.at[k], r.k1_s.at[d, k], r.k1_r.at[k], y_dev(to)))

    @pl.when(has_next)
    def _():
        start(nb)

    @pl.when(last)
    def _():
        start(k1_last)

    @pl.when(before)
    def _():
        start(k1_before)

    loads["tk"].wait()
    split_heads(r.v_tk, r.tmp, r.kh, TB, HD)
    loads["tv"].wait()
    split_heads(r.v_tv, r.tmp, r.vh, TB, HD)
    block_states(r.kh, r.vh, r.states)
    local_states(coef, r.states, r.local, r.local_bf, r.total)

    px = [send(r.total.at[rows_of(to * 256, 256), :], r.xin.at[x], r.px_s.at[d], r.px_r.at[d], x_dev(to)) for d, to in enumerate(xs)]
    start(px)
    r.xin[x] = r.total[mine_x, :]
    l1 = [send(r.local_bf.at[:, rows_of(to * 256, 256), :], r.l1, r.l1_s.at[d], r.l1_r, x_dev(to)) for d, to in enumerate(xs)]

    @pl.when(last)
    def _():
        start(l1)
        r.l1[...] = r.local_bf[:, mine_x, :]

    k2_last = [send(r.k1.at[k, pl.ds(0, 3), rows_of(to * 16, 16), :], r.kvbc.at[k, pl.ds(4, 3), rows_of(y * 64 + to * 16, 16), :],
                    r.k2_s.at[d, k], r.k2_r.at[k], x_dev(to)) for d, to in enumerate(xs) for k in range(2)]
    k2_before = [send(r.k1.at[k, :, rows_of(to * 16, 16), :], r.kvbc.at[k, pl.ds(0, 4), rows_of(y * 64 + to * 16, 16), :],
                      r.k2_s.at[d, k], r.k2_r.at[2 + k], x_dev(to)) for d, to in enumerate(xs) for k in range(2)]
    own16 = rows_of(x * 16, 16)
    loads["twk"].wait()
    loads["twv"].wait()

    def kv_stage2():
        @pl.when(last_plane & (x == NX - 1))
        def _():
            @pl.when(y == NY - 1)
            def _():
                r.k1[0, 0:3] = r.v_twk[0:3, q64(y), :]
                r.k1[1, 0:3] = r.v_twv[0:3, q64(y), :]

            @pl.when(y != NY - 1)
            def _():
                wait_recv(k1_last[:2])

            start(k2_last)
            r.kvbc[:, 4:7, q16, :] = r.k1[:, 0:3, own16, :]

        @pl.when(last_plane & (x == NX - 2))
        def _():
            @pl.when(y == NY - 1)
            def _():
                r.k1[0] = r.v_twk[:, q64(y), :]
                r.k1[1] = r.v_twv[:, q64(y), :]

            @pl.when(y != NY - 1)
            def _():
                wait_recv(k1_before[:2])

            start(k2_before)
            r.kvbc[:, 0:4, q16, :] = r.k1[:, :, own16, :]

    h0 = 2 * x
    hy = 2 * x + y // 2
    py = [send(r.rs.at[q64(to), :], r.yin.at[y], r.y_s.at[d], r.y_r.at[d], y_dev(to)) for d, to in enumerate(ys)]
    ey = [send(r.ry.at[q64(to), :], r.exin, r.ey_s.at[d], r.ey_r, y_dev(to)) for d, to in enumerate(ys)]
    l2 = [send(r.l1.at[:, q64(to), :], r.lsl, r.l2_s.at[d], r.l2_r, y_dev(to)) for d, to in enumerate(ys)]

    def prefix_x():
        wait_recv(px)
        for hh in range(2):
            hr = slice(hh * DH, (hh + 1) * DH)
            parts = [r.xin[v, hr, :].astype(F32) for v in range(NX)]
            r.rs[hr, :] = (parts[0] + parts[1]) + (parts[2] + parts[3])
        start(py)
        r.yin[y] = r.rs[q64(y), :]
        for hh in range(2):
            hr = slice(hh * DH, (hh + 1) * DH)
            parts = [r.xin[v, hr, :].astype(F32) for v in range(NX)]
            r.ry[hr, :] = fenwick4(parts, coef(h0 + hh, 3), coef(h0 + hh, 4))[3]

        @pl.when(row_y)
        def _():
            start(ey)
            r.exin[...] = r.ry[q64(y), :]

            @pl.when(x != NX - 1)
            def _():
                l1[0].wait_recv()

            start(l2)
            r.lsl[...] = r.l1[:, q64(y), :]

    pz = [send(r.zin.at[z], r.zin.at[z], r.z_s.at[d], r.z_r.at[d], z_dev(to)) for d, to in enumerate(zs)]
    ez = [send(r.ezin, r.ezin, r.ez_s.at[d], r.ez_r, z_dev(to)) for d, to in enumerate(zs)]
    k3 = [send(r.kvbc.at[:, :, q16, :], r.kvbc.at[:, :, q16, :], r.k3_s.at[d], r.k3_r, z_dev(to)) for d, to in enumerate(zs)]
    l3 = [send(r.lsl, r.lsl, r.l3_s.at[d], r.l3_r, z_dev(to)) for d, to in enumerate(zs)]

    def y_parts():
        parts = [r.yin[v] for v in range(NY)]
        return parts, fenwick4(parts, coef(hy, 5), coef(hy, 6))

    def kv_stage3():
        @pl.when(last_plane)
        def _():
            @pl.when(x != NX - 1)
            def _():
                wait_recv(k2_last[:2])

            @pl.when(x != NX - 2)
            def _():
                wait_recv(k2_before[:2])

            start(k3)

    def prefix_y():
        wait_recv(py)
        parts, cy = y_parts()
        r.zin[z] = (parts[0] + parts[1]) + (parts[2] + parts[3])
        start(pz)

        @pl.when(last_plane)
        def _():
            @pl.when(y != NY - 1)
            def _():
                ey[0].wait_recv()

            r.ezin[...] = r.exin[...] + cy[3]
            start(ez)

            @pl.when(y != NY - 1)
            def _():
                l2[0].wait_recv()

            start(l3)

    k4 = [send(r.kvbc.at[:, :, q16, :], r.kvbc.at[:, :, q16, :], r.k4_s.at[d], r.k4_r.at[d], x_dev(to)) for d, to in enumerate(xs)]

    def kv_stage4():
        @pl.when(jnp.logical_not(last_plane))
        def _():
            k3[0].wait_recv()

        start(k4)

    yr = [send(r.ysend.at[to], r.yret.at[y], r.yr_s.at[d], r.yr_r.at[d], y_dev(to)) for d, to in enumerate(ys)]
    l4 = [send(r.lsl, r.lx.at[y], r.l4_s.at[d], r.l4_r.at[d], y_dev(to)) for d, to in enumerate(ys)]

    def prefix_z():
        @pl.when(jnp.logical_not(last_plane))
        def _():
            ez[0].wait_recv()

        wait_recv(pz)
        parts, cy = y_parts()
        zp = [r.zin[v] for v in range(NZ)]
        c7, c8, c9 = coef(hy, 7), coef(hy, 8), coef(hy, 9)
        z0, z1, z2 = z & 1, (z >> 1) & 1, (z >> 2) & 1
        half = (zp[0] + zp[1]) + (zp[2] + zp[3])
        low_pair, high_pair = zp[0] + zp[1], zp[4] + zp[5]
        cz = jnp.where(z2 == 1, c9 * half, 0.0)
        cz = cz + jnp.where(z1 == 1, c8 * jnp.where(z2 == 0, low_pair, high_pair), 0.0)
        cz = cz + jnp.where(z0 == 1, c7 * r.zin[z & 6], 0.0)
        end = r.ezin[...] + (c9 * half + c8 * high_pair + c7 * zp[6])
        for v in range(NY):
            r.ysend[v, 0] = cz if cy[v] is None else cz + cy[v]
            r.ysend[v, 1] = end
        start(yr)
        r.yret[y] = r.ysend[y]

        @pl.when(jnp.logical_not(last_plane))
        def _():
            l3[0].wait_recv()

        start(l4)
        r.lx[y] = r.lsl[...]

    k5 = [send(r.k5b.at[d], r.kctx.at[:, :, q64(y), :], r.k5_s.at[d], r.k5_r.at[d], y_dev(to)) for d, to in enumerate(ys)]

    def fork_of(slot):
        return r.fk[slot, 0:1, :]

    def kv_stage5():
        wait_recv(k4)
        wait_recv(fork_copies[3:])
        forks = [fork_of(NX + to) for to in ys] + [fork_of(NX + NY)]
        for k in range(2):
            for j in range(TB):
                blocks = [r.kvbc[k, j + f, q64(y), :].astype(F32) for f in range(TB)]
                for d, f in enumerate(forks):
                    chosen = pick(f, blocks).astype(BF16)
                    if d < NY - 1:
                        r.k5b[d, k, j] = chosen
                    else:
                        r.kctx[k, j, q64(y), :] = chosen
        start(k5)

    xr = []
    for d, to in enumerate(xs):
        xr.append(send(r.xsend.at[0, to], r.cross.at[mine_x, :], r.xr_s.at[d, 0], r.xr_r.at[d, 0], x_dev(to)))
        xr.append(send(r.xsend.at[1, to], r.end.at[mine_x, :], r.xr_s.at[d, 1], r.xr_r.at[d, 1], x_dev(to)))

    def prefix_yret():
        wait_recv(yr)
        wait_recv(l4)
        wait_recv(fork_copies[:3])
        r.fk[x] = r.fk[NX + NY]
        for yy in range(NY):
            hh = yy // 2
            hr = slice(yy * 64, (yy + 1) * 64)
            parts = [r.xin[u, hr, :].astype(F32) for u in range(NX)]
            cx = fenwick4(parts, coef(h0 + hh, 3), coef(h0 + hh, 4))
            back, cross_end = r.yret[yy, 0], r.yret[yy, 1]
            ends = [cross_end] + [cross_end + r.lx[yy, f].astype(F32) for f in range(3)]
            for v in range(NX):
                r.xsend[0, v, hr, :] = (back if cx[v] is None else back + cx[v]).astype(BF16)
                r.xsend[1, v, hr, :] = pick(fork_of(v), ends).astype(BF16)
        start(xr)
        r.cross[mine_x, :] = r.xsend[0, x]
        r.end[mine_x, :] = r.xsend[1, x]

    bad = jnp.where(s == 0, TB, 0)
    tqr = r.wqh.at[:, pl.ds(0, TB * BLK), :]
    bqr = r.wqh.at[:, pl.ds(TB * BLK, BB * BLK), :]

    def branch_window(first, end):
        @pl.loop(first, end)
        def _(i):
            for g in range(KV):
                window_block(i, g, bqr, r.kb, r.vb, r.out, None, TB * BLK)

    def trunk_window(first, end):
        @pl.loop(first, end)
        def _(i):
            for g in range(KV):
                window_block(i, g, tqr, r.kt, r.vt, r.out, bad, 0)

    loads["bwk"].wait()
    loads["bwv"].wait()
    split_heads(r.v_bwk, r.tmp, r.kb, BB, KV, TB * BLK)
    split_heads(r.v_bwv, r.tmp, r.vb, BB, KV, TB * BLK)
    kv_stage2()
    loads["bwq"].wait()
    split_heads(r.v_bwq, r.tmp, r.wqh, BB, HD, TB * BLK)
    prefix_x()
    kv_stage3()
    branch_window(4, 6)
    prefix_y()
    branch_window(6, 8)
    loads["twq"].wait()
    split_heads(r.v_twq, r.tmp, r.wqh, TB, HD)

    @pl.when(has_prev)
    def _():
        wait_recv(nb)

    @pl.when(jnp.logical_not(has_prev))
    def _():
        r.kprev[...] = jnp.zeros_like(r.kprev)
        r.vprev[...] = jnp.zeros_like(r.vprev)

    flat = lambda ref: ref.reshape(4 * 256, DH)
    split_heads(flat(r.kprev), r.tmp, r.kt, TB, KV)
    split_heads(flat(r.vprev), r.tmp, r.vt, TB, KV)
    split_heads(flat(r.v_twk), r.tmp, r.kt, TB, KV, TB * BLK)
    split_heads(flat(r.v_twv), r.tmp, r.vt, TB, KV, TB * BLK)
    prefix_z()
    kv_stage4()
    trunk_window(0, 2)
    kv_stage5()
    prefix_yret()
    trunk_window(2, 4)
    loads["tq"].wait()
    split_heads(r.v_tq, r.tmp, r.qh, TB, HD)
    loads["bq"].wait()
    split_heads(r.v_bq, r.tmp, r.bqh, BB, HD)
    wait_recv(k5)
    split_heads(flat(r.kctx.at[0]), r.tmp, r.kb, TB, KV)
    split_heads(flat(r.kctx.at[1]), r.tmp, r.vb, TB, KV)
    branch_window(0, 2)
    wait_recv(xr)

    @pl.loop(0, TB)
    def _(b):
        trunk_linear_block(b, coef, r.qh, r.kh, r.vh, r.local, r.cross, r.out)

    other = (s, 1 - head)
    sst = send(r.ss_t, r.ss_to, r.ss_s.at[0], r.ss_r.at[0], other)
    ssb = send(r.ss_b, r.ss_bo, r.ss_s.at[1], r.ss_r.at[1], other)
    trunk_out = r.out.at[:, pl.ds(0, TB * BLK), :]
    branch_out = r.out.at[:, pl.ds(TB * BLK, BB * BLK), :]

    @pl.loop(0, TB)
    def _(c):
        square_sums(trunk_out, c, r.ss_t)

    sst.start()
    branch_window(2, 4)
    branch_linear(r.bqh, r.end, r.out)

    @pl.loop(0, BB)
    def _(c):
        square_sums(branch_out, c, r.ss_b)

    ssb.start()
    size = BLK * HD

    def write(buf, hbm, c, sem):
        return pltpu.make_async_copy(buf.at[rows_of(c * size, size), :], hbm.at[rows_of(c * size, size), :], sem)

    sst.wait()

    @pl.loop(0, TB)
    def _(c):
        scale_chunk(c, trunk_out, r.ss_t, r.ss_to, r.tmp, r.obuf_t)
        write(r.obuf_t, r.trunk_hbm, c, r.out_sem.at[c]).start()

    ssb.wait()

    @pl.loop(0, BB)
    def _(c):
        scale_chunk(c, branch_out, r.ss_b, r.ss_bo, r.tmp, r.obuf_b)
        write(r.obuf_b, r.branch_hbm, c, r.out_sem.at[TB + c]).start()

    wait_send(fork_copies + px + py + pz + yr + l4 + k4 + k5 + xr)

    @pl.when(has_next)
    def _():
        wait_send(nb)

    @pl.when(last)
    def _():
        wait_send(k1_last + l1)

    @pl.when(before)
    def _():
        wait_send(k1_before)

    @pl.when(last_plane & (x == NX - 1))
    def _():
        wait_send(k2_last)

    @pl.when(last_plane & (x == NX - 2))
    def _():
        wait_send(k2_before)

    @pl.when(row_y)
    def _():
        wait_send(ey + l2)

    @pl.when(last_plane)
    def _():
        wait_send(ez + k3 + l3)

    @pl.loop(0, TB)
    def _(c):
        write(r.obuf_t, r.trunk_hbm, c, r.out_sem.at[c]).wait()

    @pl.loop(0, BB)
    def _(c):
        write(r.obuf_b, r.branch_hbm, c, r.out_sem.at[TB + c]).wait()


SM = pl.BlockSpec(memory_space=pltpu.SMEM)
HBM = pl.BlockSpec(memory_space=pl.ANY)
VM = pl.BlockSpec(memory_space=pltpu.VMEM)
VMEM_LIMIT = 62 * 1024 * 1024
R = HD * DH
T = (TB + BB) * BLK


def sds(shape, dtype):
    return jax.ShapeDtypeStruct(shape, dtype)


def neighbours(x, y, z):
    group = [z * 16 + y * 4 + lax.rem(x + d, NX) for d in range(1, NX)]
    group += [z * 16 + lax.rem(y + d, NY) * 4 + x for d in range(1, NY)]
    group += [lax.rem(z + d, NZ) * 16 + y * 4 + x for d in range(1, NZ)]
    return group


def scratch_list():
    V, D = pltpu.VMEM, pltpu.SemaphoreType.DMA
    big = lambda rows: V((rows, DH), BF16)
    return dict(
        v_tk=big(4096), v_tv=big(4096), v_twk=V((4, 256, DH), BF16), v_twv=V((4, 256, DH), BF16),
        v_bwk=big(2048), v_bwv=big(2048), v_bwq=big(8192), v_twq=big(4096), v_tq=big(4096), v_bq=big(8192),
        load_sem=D((len(INPUTS),)), out_sem=D((TB + BB,)),
        tmp=V((BLK * HD, DH), F32), kh=V((HD, TB * BLK, DH), BF16), vh=V((HD, TB * BLK, DH), BF16),
        qh=V((HD, TB * BLK, DH), BF16), wqh=V((HD, T, DH), BF16), bqh=V((HD, BB * BLK, DH), BF16),
        kt=V((KV, 2 * TB * BLK, DH), BF16), vt=V((KV, 2 * TB * BLK, DH), BF16),
        kb=V((KV, T, DH), BF16), vb=V((KV, T, DH), BF16),
        out=V((HD, T, DH), F32), obuf_t=big(4096), obuf_b=big(8192),
        states=V((TB, R, DH), F32), local=V((3, R, DH), F32), local_bf=V((3, R, DH), BF16), total=V((R, DH), BF16),
        fk=V((NX + NY + 1, 8, DH), F32), kprev=V((4, 256, DH), BF16), vprev=V((4, 256, DH), BF16),
        k1=V((2, 4, 64, DH), BF16), kvbc=V((2, 7, 256, DH), BF16), k5b=V((3, 2, 4, 64, DH), BF16),
        kctx=V((2, 4, 256, DH), BF16),
        l1=V((3, 256, DH), BF16), lsl=V((3, 64, DH), BF16), lx=V((NY, 3, 64, DH), BF16),
        xin=V((NX, 256, DH), BF16), rs=V((256, DH), F32), ry=V((256, DH), F32), yin=V((NY, 64, DH), F32),
        exin=V((64, DH), F32), zin=V((NZ, 64, DH), F32), ezin=V((64, DH), F32),
        ysend=V((NY, 2, 64, DH), F32), yret=V((NY, 2, 64, DH), F32),
        xsend=V((2, NX, 256, DH), BF16), cross=V((R, DH), BF16), end=V((R, DH), BF16),
        ss_t=V((8, DH), F32), ss_b=V((8, DH), F32), ss_to=V((8, DH), F32), ss_bo=V((8, DH), F32),
        fk_s=D((6,)), fk_r=D((6,)), nb_s=D((2,)), nb_r=D((2,)), k1_s=D((3, 2)), k1_r=D((2,)),
        px_s=D((3,)), px_r=D((3,)), l1_s=D((3,)), l1_r=D, k2_s=D((3, 2)), k2_r=D((4,)),
        y_s=D((3,)), y_r=D((3,)), ey_s=D((3,)), ey_r=D, l2_s=D((3,)), l2_r=D,
        z_s=D((7,)), z_r=D((7,)), ez_s=D((7,)), ez_r=D, k3_s=D((7,)), k3_r=D, l3_s=D((7,)), l3_r=D,
        k4_s=D((3,)), k4_r=D((3,)), yr_s=D((3,)), yr_r=D((3,)), l4_s=D((3,)), l4_r=D((3,)),
        k5_s=D((3,)), k5_r=D((3,)), xr_s=D((3, 2)), xr_r=D((3, 2)), ss_s=D((2,)), ss_r=D((2,)))


def shards(tq, tk, tv, twq, twk, twv, bq, bwq, bwk, bwv, gain, fork):
    flat = lambda a: a.reshape(-1, DH)
    blocks = lambda a: a.reshape(TB, KV * BLK, DH)
    scratch = scratch_list()
    names = ("gain", "fork") + INPUTS + ("trunk_hbm", "branch_hbm") + tuple(scratch)
    trunk_out, branch_out = pl.pallas_call(
        functools.partial(fused_kernel, names), name="fused",
        out_shape=(sds((TB * BLK * HD, DH), BF16), sds((BB * BLK * HD, DH), BF16)),
        in_specs=[SM, SM] + [HBM] * len(INPUTS), out_specs=(HBM, HBM),
        scratch_shapes=list(scratch.values()),
        compiler_params=pltpu.CompilerParams(vmem_limit_bytes=VMEM_LIMIT, collective_id=0, has_side_effects=True),
    )(gain, fork, flat(tk), flat(tv), blocks(twk), blocks(twv), flat(bwk), flat(bwv), flat(bwq), flat(twq), flat(tq), flat(bq))
    return trunk_out.reshape(TB * BLK, HD, DH), branch_out.reshape(BB * BLK, HD, DH)


def solution(mesh):
    spec = P("seq", "head", None)
    return jax.shard_map(
        shards, mesh=mesh, in_specs=(spec,) * 10 + (P("head", None), P("seq")),
        out_specs=(spec, spec), check_vma=False)
```

```python
import functools
import math

import jax
import jax.numpy as jnp
from jax import lax
from jax.experimental import pallas as pl
from jax.experimental.pallas import tpu as pltpu
from jax.sharding import PartitionSpec as P

F32, BF16 = jnp.float32, jnp.bfloat16
MESH = pl.DeviceIdType.MESH
DH = 128
BLK = 128
HD = 8
KV = 2
TB = 4
BB = 8
NP, NZ = 16, 8
NEG = -1e30
EXP2_SCALE = math.log2(math.e) / math.sqrt(DH)
NT = (((1,), (1,)), ((), ()))
NN = (((1,), (0,)), ((), ()))
TN = (((0,), (0,)), ((), ()))


def dot(a, b, dims=NN):
    return lax.dot_general(a, b, dims, preferred_element_type=F32)


def rows_of(start, size):
    return pl.ds(pl.multiple_of(start, size), size)


def split_heads(src, tmp, dst, chunks, heads, dst_start=0):
    size = BLK * heads

    @pl.loop(0, chunks)
    def _(c):
        rows = src[rows_of(c * size, size), :].reshape(BLK, heads, DH)
        dst[:, rows_of(c * BLK + dst_start, BLK), :] = jnp.swapaxes(rows, 0, 1)


def level_weight(gain, h, level):
    return gain[h, level] * (1.0 / math.sqrt(DH * BLK * 2 ** max(level - 1, 0)))


def block_states(kh, vh, states):
    @pl.loop(0, TB)
    def _(b):
        rows = rows_of(b * BLK, BLK)
        for h in range(HD):
            states[b, h * DH : (h + 1) * DH, :] = dot(kh[h, rows, :], vh[h, rows, :], TN)


def local_states(coef, states, local, local_bf, total_bf):
    for h in range(HD):
        rows = slice(h * DH, (h + 1) * DH)
        c1, c2 = coef(h, 1), coef(h, 2)
        s0, s1, s2, s3 = (states[b, rows, :] for b in range(TB))
        two = c2 * (s0 + s1)
        parts = (c1 * s0, two, two + c1 * s2)
        for f, part in enumerate(parts):
            local[f, rows, :] = part
            local_bf[f, rows, :] = part.astype(BF16)
        total_bf[rows, :] = ((s0 + s1) + (s2 + s3)).astype(BF16)


def window_block(i, g, qh, kw, vw, out, bad_below, out_start):
    keys = kw[g, pl.ds(pl.multiple_of(i * BLK, BLK), 5 * BLK), :]
    values = vw[g, pl.ds(pl.multiple_of(i * BLK, BLK), 5 * BLK), :]
    rows = rows_of(i * BLK, BLK)
    q = qh[4 * g : 4 * g + 4, rows, :].reshape(4 * BLK, DH)
    s = dot(q, keys, NT)
    row = lax.broadcasted_iota(jnp.int32, (4 * BLK, BLK), 0) & (BLK - 1)
    col = lax.broadcasted_iota(jnp.int32, (4 * BLK, BLK), 1)
    own = col <= row
    tiles = [s[:, j * BLK : (j + 1) * BLK] for j in range(5)]
    if bad_below is not None:
        for j in range(4):
            tiles[j] = jnp.where(i + j < bad_below, NEG, tiles[j])
    tiles = [jnp.where(own, tiles[4], tiles[0])] + tiles[1:4]
    top = jnp.maximum(jnp.maximum(tiles[0], tiles[1]), jnp.maximum(tiles[2], tiles[3]))
    top = jnp.max(top, axis=-1, keepdims=True) * EXP2_SCALE
    ex = [jnp.exp2(t * EXP2_SCALE - top) for t in tiles]
    total = jnp.sum((ex[0] + ex[1]) + (ex[2] + ex[3]), axis=-1, keepdims=True)
    inv = 1.0 / total
    edge = ex[0] * inv
    pieces = [jnp.where(own, 0.0, edge).astype(BF16)]
    pieces += [(e * inv).astype(BF16) for e in ex[1:]]
    pieces += [jnp.where(own, edge, 0.0).astype(BF16)]
    o = dot(jnp.concatenate(pieces, axis=1), values)
    out[4 * g : 4 * g + 4, rows_of(out_start + i * BLK, BLK), :] = o.reshape(4, BLK, DH)


def trunk_linear_block(b, coef, qh, kh, vh, local, cross, out):
    rows = rows_of(b * BLK, BLK)
    row = lax.broadcasted_iota(jnp.int32, (BLK, BLK), 0)
    col = lax.broadcasted_iota(jnp.int32, (BLK, BLK), 1)
    for h in range(HD):
        hr = slice(h * DH, (h + 1) * DH)
        q = qh[h, rows, :]
        s = dot(q, kh[h, rows, :], NT)
        w = jnp.where(col <= row, s * coef(h, 0), 0.0).astype(BF16)
        loc = jnp.where(b == 0, 0.0, local[jnp.maximum(b - 1, 0), hr, :])
        combined = (cross[hr, :].astype(F32) + loc).astype(BF16)
        out[h, rows, :] = out[h, rows, :] + (dot(w, vh[h, rows, :]) + dot(q, combined))


def square_sums(out, chunk, ss):
    acc = None
    for h in range(HD):
        o = out[h, rows_of(chunk * BLK, BLK), :]
        acc = o * o if acc is None else acc + o * o
    ss[pl.ds(chunk, 1), :] = jnp.sum(acc.T, axis=0, keepdims=True)


def branch_linear(bqh, end, out):
    @pl.loop(0, HD)
    def _(h):
        er = end[rows_of(h * DH, DH), :]
        for c in range(2):
            src = slice(c * 512, (c + 1) * 512)
            dst = slice(TB * BLK + c * 512, TB * BLK + (c + 1) * 512)
            out[h, dst, :] = out[h, dst, :] + dot(bqh[h, src, :], er)


def scale_chunk(c, out, ss_own, ss_other, tmp, obuf):
    total = ss_own[pl.ds(c, 1), :] + ss_other[pl.ds(c, 1), :]
    r = lax.rsqrt(total / (2 * HD * DH) + 1e-6)
    scale = jnp.broadcast_to(r, (BLK, BLK)).T
    for h in range(HD):
        tmp[pl.ds(h, BLK, stride=HD), :] = out[h, rows_of(c * BLK, BLK), :] * scale
    obuf[rows_of(c * BLK * HD, BLK * HD), :] = tmp[...].astype(BF16)


def prefix16(parts, weights):
    sums = [parts]
    for _ in range(3):
        low = sums[-1]
        sums.append([low[i] + low[i + 1] for i in range(0, len(low), 2)])
    total = sums[3][0] + sums[3][1]

    def prefix(v):
        acc = None
        for bit in range(4):
            if v >> bit & 1:
                term = weights[bit] * sums[bit][(v >> bit) - 1]
                acc = term if acc is None else acc + term
        return acc

    return total, prefix


def pick(f, options):
    chosen = options[0]
    for k in range(1, len(options)):
        chosen = jnp.where(f == k, options[k], chosen)
    return chosen


INPUTS = ("tk", "tv", "twk", "twv", "bwk", "bwv", "bwq", "twq", "tq", "bq")


class Refs:
    pass


def fused_kernel(names, *refs):
    r = Refs()
    for name, ref in zip(names, refs):
        setattr(r, name, ref)
    coef = functools.partial(level_weight, r.gain)
    s = lax.axis_index("seq")
    head = lax.axis_index("head")
    n = NP * NZ
    p, z = lax.rem(s, NP), s // NP
    wrap = lax.rem

    loads = {}
    for k, name in enumerate(INPUTS):
        loads[name] = pltpu.make_async_copy(getattr(r, name), getattr(r, "v_" + name), r.load_sem.at[k])
        loads[name].start()

    ps = [wrap(p + d, NP) for d in range(1, NP)]
    zs = [wrap(z + d, NZ) for d in range(1, NZ)]
    barrier = pltpu.get_barrier_semaphore()
    peers = [(z * NP + v, head) for v in ps] + [(v * NP + p, head) for v in zs]
    peers += [(wrap(s + 1, n), head), (wrap(s + n - 1, n), head), (s, 1 - head)]
    for peer in peers:
        pl.semaphore_signal(barrier, inc=1, device_id=peer, device_id_type=MESH)
    r.fk[NP] = jnp.full((8, DH), r.fork[0], jnp.int32).astype(F32)
    pl.semaphore_wait(barrier, len(peers))

    def send(src, dst, ssem, rsem, to):
        return pltpu.make_async_remote_copy(
            src_ref=src, dst_ref=dst, send_sem=ssem, recv_sem=rsem, device_id=to, device_id_type=MESH)

    def in_plane(v):
        return (z * NP + v, head)

    def in_column(v):
        return (v * NP + p, head)

    has_prev, has_next = s > 0, s < n - 1
    last, before = s == n - 1, s == n - 2
    last_plane = z == NZ - 1
    q64 = lambda v: rows_of(v * 64, 64)
    q16 = lambda v: rows_of(v * 16, 16)

    def start(copies):
        for c in copies:
            c.start()

    def wait_send(copies):
        for c in copies:
            c.wait_send()

    def wait_recv(copies):
        for c in copies:
            c.wait_recv()

    forks = [send(r.fk.at[NP], r.fk.at[p], r.fk_s.at[d], r.fk_r.at[d], in_plane(to)) for d, to in enumerate(ps)]
    nxt = (jnp.minimum(s + 1, n - 1), head)
    nb = [send(a, b, r.nb_s.at[k], r.nb_r.at[k], nxt) for k, (a, b) in enumerate(((r.twk, r.kprev), (r.twv, r.vprev)))]

    k1_last, k1_before = [], []
    for d, to in enumerate(ps):
        for k, src in enumerate((r.twk, r.twv)):
            k1_last.append(send(src.at[pl.ds(0, 3), q16(to), :], r.ksl.at[k, pl.ds(4, 3)], r.k1_s.at[d, k], r.k1_r.at[k], in_plane(to)))
            k1_before.append(send(src.at[:, q16(to), :], r.ksl.at[k, pl.ds(0, 4)], r.k1_s.at[d, k], r.k1_r.at[2 + k], in_plane(to)))

    @pl.when(last)
    def _():
        start(k1_last)

    @pl.when(before)
    def _():
        start(k1_before)

    start(forks)

    @pl.when(has_next)
    def _():
        nb[0].start()

    loads["tk"].wait()
    split_heads(r.v_tk, r.tmp, r.kh, TB, HD)
    loads["tv"].wait()
    split_heads(r.v_tv, r.tmp, r.vh, TB, HD)
    block_states(r.kh, r.vh, r.states)
    local_states(coef, r.states, r.local, r.local_bf, r.total)

    pa = [send(r.total.at[q64(to), :], r.xin.at[p], r.pa_s.at[d], r.pa_r.at[d], in_plane(to)) for d, to in enumerate(ps)]
    start(pa)
    r.xin[p] = r.total[q64(p), :]
    l1 = [send(r.local_bf.at[:, q64(to), :], r.lsl, r.l1_s.at[d], r.l1_r, in_plane(to)) for d, to in enumerate(ps)]

    @pl.when(last)
    def _():
        start(l1)
        r.lsl[...] = r.local_bf[:, q64(p), :]

    k3 = [send(r.ksl, r.ksl, r.k3_s.at[d], r.k3_r, in_column(to)) for d, to in enumerate(zs)]
    l3 = [send(r.lsl, r.lsl, r.l3_s.at[d], r.l3_r, in_column(to)) for d, to in enumerate(zs)]
    pz = [send(r.zin.at[z], r.zin.at[z], r.z_s.at[d], r.z_r.at[d], in_column(to)) for d, to in enumerate(zs)]
    ez = [send(r.ezin, r.ezin, r.ez_s.at[d], r.ez_r, in_column(to)) for d, to in enumerate(zs)]
    loads["twk"].wait()
    loads["twv"].wait()

    def context_to_planes():
        @pl.when(last_plane)
        def _():
            @pl.when(last)
            def _():
                for k, src in enumerate((r.v_twk, r.v_twv)):
                    r.ksl[k, 4:7] = src[0:3, q16(p), :]

            @pl.when(before)
            def _():
                for k, src in enumerate((r.v_twk, r.v_twv)):
                    r.ksl[k, 0:4] = src[:, q16(p), :]

            @pl.when(jnp.logical_not(last))
            def _():
                wait_recv(k1_last[:2])

            @pl.when(jnp.logical_not(before))
            def _():
                wait_recv(k1_before[:2])

            start(k3)

    hp = p // 2

    def plane_parts():
        parts = [r.xin[v].astype(F32) for v in range(NP)]
        return prefix16(parts, [coef(hp, level) for level in range(3, 7)])

    def prefix_plane():
        wait_recv(pa)
        total, prefix = plane_parts()
        r.zin[z] = total.astype(BF16)
        start(pz)

        @pl.when(last_plane)
        def _():
            r.ezin[...] = prefix(NP - 1).astype(BF16)
            start(ez)

    def local_to_planes():
        @pl.when(last_plane)
        def _():
            @pl.when(jnp.logical_not(last))
            def _():
                l1[0].wait_recv()

            start(l3)

    k5 = [send(r.kout.at[to], r.kctx.at[:, :, q16(p), :], r.k5_s.at[d], r.k5_r.at[d], in_plane(to)) for d, to in enumerate(ps)]

    def fork_of(v):
        return r.fk[v, 0:1, :]

    def context_back():
        @pl.when(jnp.logical_not(last_plane))
        def _():
            k3[0].wait_recv()

        wait_recv(forks)
        r.fk[p] = r.fk[NP]
        for k in range(2):
            for j in range(TB):
                blocks = [r.ksl[k, j + f].astype(F32) for f in range(TB)]
                for v in range(NP):
                    r.kout[v, k, j] = pick(fork_of(v), blocks).astype(BF16)
        start(k5)
        r.kctx[:, :, q16(p), :] = r.kout[p]

    xr = [send(r.rsend.at[to], r.cross.at[q64(p), :], r.xr_s.at[d], r.xr_r.at[d], in_plane(to)) for d, to in enumerate(ps)]
    xe = [send(r.esend.at[to], r.end.at[q64(p), :], r.xe_s.at[d], r.xe_r.at[d], in_plane(to)) for d, to in enumerate(ps)]

    def prefix_back():
        @pl.when(jnp.logical_not(last_plane))
        def _():
            ez[0].wait_recv()

        wait_recv(pz)
        zp = [r.zin[v].astype(F32) for v in range(NZ)]
        c7, c8, c9 = coef(hp, 7), coef(hp, 8), coef(hp, 9)
        z0, z1, z2 = z & 1, (z >> 1) & 1, (z >> 2) & 1
        half = (zp[0] + zp[1]) + (zp[2] + zp[3])
        low_pair, high_pair = zp[0] + zp[1], zp[4] + zp[5]
        cz = jnp.where(z2 == 1, c9 * half, 0.0)
        cz = cz + jnp.where(z1 == 1, c8 * jnp.where(z2 == 0, low_pair, high_pair), 0.0)
        cz = cz + jnp.where(z0 == 1, c7 * r.zin[z & 6].astype(F32), 0.0)
        r.ecross[...] = r.ezin[...].astype(F32) + (c9 * half + c8 * high_pair + c7 * zp[6])
        _, prefix = plane_parts()
        for v in range(NP):
            own = prefix(v)
            r.rsend[v] = (cz if own is None else cz + own).astype(BF16)
        start(xr)
        r.cross[q64(p), :] = r.rsend[p]

    def ends_back():
        @pl.when(jnp.logical_not(last_plane))
        def _():
            l3[0].wait_recv()

        base = r.ecross[...]
        ends = [base] + [base + r.lsl[f].astype(F32) for f in range(3)]
        for v in range(NP):
            r.esend[v] = pick(fork_of(v), ends).astype(BF16)
        start(xe)
        r.end[q64(p), :] = r.esend[p]

    bad = jnp.where(s == 0, TB, 0)
    tqr = r.wqh.at[:, pl.ds(0, TB * BLK), :]
    bqr = r.wqh.at[:, pl.ds(TB * BLK, BB * BLK), :]

    def branch_window(first, end):
        @pl.loop(first, end)
        def _(i):
            for g in range(KV):
                window_block(i, g, bqr, r.kb, r.vb, r.out, None, TB * BLK)

    def trunk_window(first, end):
        @pl.loop(first, end)
        def _(i):
            for g in range(KV):
                window_block(i, g, tqr, r.kt, r.vt, r.out, bad, 0)

    loads["bwk"].wait()
    loads["bwv"].wait()
    split_heads(r.v_bwk, r.tmp, r.kb, BB, KV, TB * BLK)
    split_heads(r.v_bwv, r.tmp, r.vb, BB, KV, TB * BLK)
    loads["bwq"].wait()
    split_heads(r.v_bwq, r.tmp, r.wqh, BB, HD, TB * BLK)
    context_to_planes()
    branch_window(4, 6)
    prefix_plane()

    @pl.when(has_next)
    def _():
        nb[1].start()

    branch_window(6, 7)
    local_to_planes()
    branch_window(7, 8)
    context_back()
    loads["twq"].wait()
    split_heads(r.v_twq, r.tmp, r.wqh, TB, HD)

    @pl.when(has_prev)
    def _():
        wait_recv(nb)

    @pl.when(jnp.logical_not(has_prev))
    def _():
        r.kprev[...] = jnp.zeros_like(r.kprev)
        r.vprev[...] = jnp.zeros_like(r.vprev)

    flat = lambda ref: ref.reshape(4 * 256, DH)
    split_heads(flat(r.kprev), r.tmp, r.kt, TB, KV)
    split_heads(flat(r.vprev), r.tmp, r.vt, TB, KV)
    split_heads(flat(r.v_twk), r.tmp, r.kt, TB, KV, TB * BLK)
    split_heads(flat(r.v_twv), r.tmp, r.vt, TB, KV, TB * BLK)
    trunk_window(0, 1)
    prefix_back()
    trunk_window(1, 4)
    ends_back()
    loads["tq"].wait()
    split_heads(r.v_tq, r.tmp, r.qh, TB, HD)
    loads["bq"].wait()
    split_heads(r.v_bq, r.tmp, r.bqh, BB, HD)
    wait_recv(k5)
    split_heads(flat(r.kctx.at[0]), r.tmp, r.kb, TB, KV)
    split_heads(flat(r.kctx.at[1]), r.tmp, r.vb, TB, KV)
    branch_window(0, 2)
    wait_recv(xr)

    @pl.loop(0, TB)
    def _(b):
        trunk_linear_block(b, coef, r.qh, r.kh, r.vh, r.local, r.cross, r.out)

    other = (s, 1 - head)
    sst = send(r.ss_t, r.ss_to, r.ss_s.at[0], r.ss_r.at[0], other)
    ssb = send(r.ss_b, r.ss_bo, r.ss_s.at[1], r.ss_r.at[1], other)
    trunk_out = r.out.at[:, pl.ds(0, TB * BLK), :]
    branch_out = r.out.at[:, pl.ds(TB * BLK, BB * BLK), :]

    @pl.loop(0, TB)
    def _(c):
        square_sums(trunk_out, c, r.ss_t)

    sst.start()
    branch_window(2, 4)
    wait_recv(xe)
    branch_linear(r.bqh, r.end, r.out)

    @pl.loop(0, BB)
    def _(c):
        square_sums(branch_out, c, r.ss_b)

    ssb.start()
    size = BLK * HD

    def write(buf, hbm, c, sem):
        return pltpu.make_async_copy(buf.at[rows_of(c * size, size), :], hbm.at[rows_of(c * size, size), :], sem)

    sst.wait()

    @pl.loop(0, TB)
    def _(c):
        scale_chunk(c, trunk_out, r.ss_t, r.ss_to, r.tmp, r.obuf_t)
        write(r.obuf_t, r.trunk_hbm, c, r.out_sem.at[c]).start()

    ssb.wait()

    @pl.loop(0, BB)
    def _(c):
        scale_chunk(c, branch_out, r.ss_b, r.ss_bo, r.tmp, r.obuf_b)
        write(r.obuf_b, r.branch_hbm, c, r.out_sem.at[TB + c]).start()

    wait_send(forks + pa + pz + k5 + xr + xe)

    @pl.when(has_next)
    def _():
        wait_send(nb)

    @pl.when(last)
    def _():
        wait_send(k1_last + l1)

    @pl.when(before)
    def _():
        wait_send(k1_before)

    @pl.when(last_plane)
    def _():
        wait_send(ez + k3 + l3)

    @pl.loop(0, TB)
    def _(c):
        write(r.obuf_t, r.trunk_hbm, c, r.out_sem.at[c]).wait()

    @pl.loop(0, BB)
    def _(c):
        write(r.obuf_b, r.branch_hbm, c, r.out_sem.at[TB + c]).wait()


SM = pl.BlockSpec(memory_space=pltpu.SMEM)
HBM = pl.BlockSpec(memory_space=pl.ANY)
VM = pl.BlockSpec(memory_space=pltpu.VMEM)
VMEM_LIMIT = 62 * 1024 * 1024
R = HD * DH
T = (TB + BB) * BLK


def sds(shape, dtype):
    return jax.ShapeDtypeStruct(shape, dtype)


def scratch_list():
    V, D = pltpu.VMEM, pltpu.SemaphoreType.DMA
    big = lambda rows: V((rows, DH), BF16)
    return dict(
        v_tk=big(4096), v_tv=big(4096), v_twk=V((4, 256, DH), BF16), v_twv=V((4, 256, DH), BF16),
        v_bwk=big(2048), v_bwv=big(2048), v_bwq=big(8192), v_twq=big(4096), v_tq=big(4096), v_bq=big(8192),
        load_sem=D((len(INPUTS),)), out_sem=D((TB + BB,)),
        tmp=V((BLK * HD, DH), F32), kh=V((HD, TB * BLK, DH), BF16), vh=V((HD, TB * BLK, DH), BF16),
        qh=V((HD, TB * BLK, DH), BF16), wqh=V((HD, T, DH), BF16), bqh=V((HD, BB * BLK, DH), BF16),
        kt=V((KV, 2 * TB * BLK, DH), BF16), vt=V((KV, 2 * TB * BLK, DH), BF16),
        kb=V((KV, T, DH), BF16), vb=V((KV, T, DH), BF16),
        out=V((HD, T, DH), F32), obuf_t=big(4096), obuf_b=big(8192),
        states=V((TB, R, DH), F32), local=V((3, R, DH), F32), local_bf=V((3, R, DH), BF16), total=V((R, DH), BF16),
        fk=V((NP + 1, 8, DH), F32), kprev=V((4, 256, DH), BF16), vprev=V((4, 256, DH), BF16),
        ksl=V((2, 7, 16, DH), BF16), kout=V((NP, 2, 4, 16, DH), BF16), kctx=V((2, 4, 256, DH), BF16),
        lsl=V((3, 64, DH), BF16), xin=V((NP, 64, DH), BF16), zin=V((NZ, 64, DH), BF16), ezin=V((64, DH), BF16),
        ecross=V((64, DH), F32), rsend=V((NP, 64, DH), BF16), esend=V((NP, 64, DH), BF16),
        cross=V((R, DH), BF16), end=V((R, DH), BF16),
        ss_t=V((8, DH), F32), ss_b=V((8, DH), F32), ss_to=V((8, DH), F32), ss_bo=V((8, DH), F32),
        fk_s=D((15,)), fk_r=D((15,)), nb_s=D((2,)), nb_r=D((2,)), k1_s=D((15, 2)), k1_r=D((4,)),
        pa_s=D((15,)), pa_r=D((15,)), l1_s=D((15,)), l1_r=D, z_s=D((7,)), z_r=D((7,)), ez_s=D((7,)), ez_r=D,
        k3_s=D((7,)), k3_r=D, l3_s=D((7,)), l3_r=D, k5_s=D((15,)), k5_r=D((15,)),
        xr_s=D((15,)), xr_r=D((15,)), xe_s=D((15,)), xe_r=D((15,)), ss_s=D((2,)), ss_r=D((2,)))


def shards(tq, tk, tv, twq, twk, twv, bq, bwq, bwk, bwv, gain, fork):
    flat = lambda a: a.reshape(-1, DH)
    blocks = lambda a: a.reshape(TB, KV * BLK, DH)
    scratch = scratch_list()
    names = ("gain", "fork") + INPUTS + ("trunk_hbm", "branch_hbm") + tuple(scratch)
    trunk_out, branch_out = pl.pallas_call(
        functools.partial(fused_kernel, names), name="fused",
        out_shape=(sds((TB * BLK * HD, DH), BF16), sds((BB * BLK * HD, DH), BF16)),
        in_specs=[SM, SM] + [HBM] * len(INPUTS), out_specs=(HBM, HBM),
        scratch_shapes=list(scratch.values()),
        compiler_params=pltpu.CompilerParams(vmem_limit_bytes=VMEM_LIMIT, collective_id=0, has_side_effects=True),
    )(gain, fork, flat(tk), flat(tv), blocks(twk), blocks(twv), flat(bwk), flat(bwv), flat(bwq), flat(twq), flat(tq), flat(bq))
    return trunk_out.reshape(TB * BLK, HD, DH), branch_out.reshape(BB * BLK, HD, DH)


def solution(mesh):
    spec = P("seq", "head", None)
    return jax.shard_map(
        shards, mesh=mesh, in_specs=(spec,) * 10 + (P("head", None), P("seq")),
        out_specs=(spec, spec), check_vma=False)
```

```python
import functools
import math

import jax
import jax.numpy as jnp
from jax import lax
from jax.experimental import pallas as pl
from jax.experimental.pallas import tpu as pltpu
from jax.sharding import PartitionSpec as P

F32, BF16 = jnp.float32, jnp.bfloat16
MESH = pl.DeviceIdType.MESH
DH = 128
BLK = 128
HD = 8
KV = 2
TB = 4
BB = 8
NP, NZ = 16, 8
NEG = -1e30
EXP2_SCALE = math.log2(math.e) / math.sqrt(DH)
NT = (((1,), (1,)), ((), ()))
NN = (((1,), (0,)), ((), ()))
TN = (((0,), (0,)), ((), ()))


def dot(a, b, dims=NN):
    return lax.dot_general(a, b, dims, preferred_element_type=F32)


def rows_of(start, size):
    return pl.ds(pl.multiple_of(start, size), size)


def split_heads(src, tmp, dst, chunks, heads, dst_start=0):
    size = BLK * heads

    @pl.loop(0, chunks)
    def _(c):
        rows = src[rows_of(c * size, size), :].reshape(BLK, heads, DH)
        dst[:, rows_of(c * BLK + dst_start, BLK), :] = jnp.swapaxes(rows, 0, 1)


def level_weight(gain, h, level):
    return gain[h, level] * (1.0 / math.sqrt(DH * BLK * 2 ** max(level - 1, 0)))


def block_states(kh, vh, states):
    @pl.loop(0, TB)
    def _(b):
        rows = rows_of(b * BLK, BLK)
        for h in range(HD):
            states[b, h * DH : (h + 1) * DH, :] = dot(kh[h, rows, :], vh[h, rows, :], TN)


def local_states(coef, states, local, local_bf, total_bf):
    for h in range(HD):
        rows = slice(h * DH, (h + 1) * DH)
        c1, c2 = coef(h, 1), coef(h, 2)
        s0, s1, s2, s3 = (states[b, rows, :] for b in range(TB))
        two = c2 * (s0 + s1)
        parts = (c1 * s0, two, two + c1 * s2)
        for f, part in enumerate(parts):
            local[f, rows, :] = part
            local_bf[f, rows, :] = part.astype(BF16)
        total_bf[rows, :] = ((s0 + s1) + (s2 + s3)).astype(BF16)


def window_block(i, g, qh, kw, vw, out, bad_below, out_start):
    keys = kw[g, pl.ds(pl.multiple_of(i * BLK, BLK), 5 * BLK), :]
    values = vw[g, pl.ds(pl.multiple_of(i * BLK, BLK), 5 * BLK), :]
    rows = rows_of(i * BLK, BLK)
    q = qh[4 * g : 4 * g + 4, rows, :].reshape(4 * BLK, DH)
    s = dot(q, keys, NT)
    row = lax.broadcasted_iota(jnp.int32, (4 * BLK, BLK), 0) & (BLK - 1)
    col = lax.broadcasted_iota(jnp.int32, (4 * BLK, BLK), 1)
    own = col <= row
    tiles = [s[:, j * BLK : (j + 1) * BLK] for j in range(5)]
    if bad_below is not None:
        for j in range(4):
            tiles[j] = jnp.where(i + j < bad_below, NEG, tiles[j])
    tiles = [jnp.where(own, tiles[4], tiles[0])] + tiles[1:4]
    top = jnp.maximum(jnp.maximum(tiles[0], tiles[1]), jnp.maximum(tiles[2], tiles[3]))
    top = jnp.max(top, axis=-1, keepdims=True) * EXP2_SCALE
    ex = [jnp.exp2(t * EXP2_SCALE - top) for t in tiles]
    total = jnp.sum((ex[0] + ex[1]) + (ex[2] + ex[3]), axis=-1, keepdims=True)
    pieces = [jnp.where(own, 0.0, ex[0]).astype(BF16)]
    pieces += [e.astype(BF16) for e in ex[1:]]
    pieces += [jnp.where(own, ex[0], 0.0).astype(BF16)]
    o = dot(jnp.concatenate(pieces, axis=1), values) * (1.0 / total)
    out[4 * g : 4 * g + 4, rows_of(out_start + i * BLK, BLK), :] = o.reshape(4, BLK, DH)


def trunk_linear_block(b, coef, qh, kh, vh, local, cross, out):
    rows = rows_of(b * BLK, BLK)
    row = lax.broadcasted_iota(jnp.int32, (BLK, BLK), 0)
    col = lax.broadcasted_iota(jnp.int32, (BLK, BLK), 1)
    for h in range(HD):
        hr = slice(h * DH, (h + 1) * DH)
        q = qh[h, rows, :]
        s = dot(q, kh[h, rows, :], NT)
        w = jnp.where(col <= row, s * coef(h, 0), 0.0).astype(BF16)
        loc = jnp.where(b == 0, 0.0, local[jnp.maximum(b - 1, 0), hr, :])
        combined = (cross[hr, :].astype(F32) + loc).astype(BF16)
        out[h, rows, :] = out[h, rows, :] + (dot(w, vh[h, rows, :]) + dot(q, combined))


def square_sums(out, chunk, ss):
    acc = None
    for h in range(HD):
        o = out[h, rows_of(chunk * BLK, BLK), :]
        acc = o * o if acc is None else acc + o * o
    ss[pl.ds(chunk, 1), :] = jnp.sum(acc.T, axis=0, keepdims=True)


def branch_linear(bqh, end, out):
    @pl.loop(0, HD)
    def _(h):
        er = end[rows_of(h * DH, DH), :]
        for c in range(2):
            src = slice(c * 512, (c + 1) * 512)
            dst = slice(TB * BLK + c * 512, TB * BLK + (c + 1) * 512)
            out[h, dst, :] = out[h, dst, :] + dot(bqh[h, src, :], er)


def scale_chunk(c, out, ss_own, ss_other, tmp, obuf):
    total = ss_own[pl.ds(c, 1), :] + ss_other[pl.ds(c, 1), :]
    r = lax.rsqrt(total / (2 * HD * DH) + 1e-6)
    scale = jnp.broadcast_to(r, (BLK, BLK)).T
    for h in range(HD):
        tmp[pl.ds(h, BLK, stride=HD), :] = out[h, rows_of(c * BLK, BLK), :] * scale
    obuf[rows_of(c * BLK * HD, BLK * HD), :] = tmp[...].astype(BF16)


def prefix16(parts, weights):
    sums = [parts]
    for _ in range(3):
        low = sums[-1]
        sums.append([low[i] + low[i + 1] for i in range(0, len(low), 2)])
    total = sums[3][0] + sums[3][1]

    def prefix(v):
        acc = None
        for bit in range(4):
            if v >> bit & 1:
                term = weights[bit] * sums[bit][(v >> bit) - 1]
                acc = term if acc is None else acc + term
        return acc

    return total, prefix


def pick(f, options):
    chosen = options[0]
    for k in range(1, len(options)):
        chosen = jnp.where(f == k, options[k], chosen)
    return chosen


INPUTS = ("tk", "tv", "twk", "twv", "bwk", "bwv", "bwq", "twq", "tq", "bq")


class Refs:
    pass


def fused_kernel(names, *refs):
    r = Refs()
    for name, ref in zip(names, refs):
        setattr(r, name, ref)
    coef = functools.partial(level_weight, r.gain)
    s = lax.axis_index("seq")
    head = lax.axis_index("head")
    n = NP * NZ
    p, z = lax.rem(s, NP), s // NP
    wrap = lax.rem

    loads = {}
    for k, name in enumerate(INPUTS):
        loads[name] = pltpu.make_async_copy(getattr(r, name), getattr(r, "v_" + name), r.load_sem.at[k])
        loads[name].start()

    ps = [wrap(p + d, NP) for d in range(1, NP)]
    zs = [wrap(z + d, NZ) for d in range(1, NZ)]
    barrier = pltpu.get_barrier_semaphore()
    peers = [(z * NP + v, head) for v in ps] + [(v * NP + p, head) for v in zs]
    peers += [(wrap(s + 1, n), head), (wrap(s + n - 1, n), head), (s, 1 - head)]
    for peer in peers:
        pl.semaphore_signal(barrier, inc=1, device_id=peer, device_id_type=MESH)
    r.fk[NP] = jnp.full((8, DH), r.fork[0], jnp.int32).astype(F32)
    pl.semaphore_wait(barrier, len(peers))

    def send(src, dst, ssem, rsem, to):
        return pltpu.make_async_remote_copy(
            src_ref=src, dst_ref=dst, send_sem=ssem, recv_sem=rsem, device_id=to, device_id_type=MESH)

    def in_plane(v):
        return (z * NP + v, head)

    def in_column(v):
        return (v * NP + p, head)

    has_prev, has_next = s > 0, s < n - 1
    last, before = s == n - 1, s == n - 2
    last_plane = z == NZ - 1
    q64 = lambda v: rows_of(v * 64, 64)
    q16 = lambda v: rows_of(v * 16, 16)

    def start(copies):
        for c in copies:
            c.start()

    def wait_send(copies):
        for c in copies:
            c.wait_send()

    def wait_recv(copies):
        for c in copies:
            c.wait_recv()

    forks = [send(r.fk.at[NP], r.fk.at[p], r.fk_s.at[d], r.fk_r.at[d], in_plane(to)) for d, to in enumerate(ps)]
    nxt = (jnp.minimum(s + 1, n - 1), head)
    nb = [send(a, b, r.nb_s.at[k], r.nb_r.at[k], nxt) for k, (a, b) in enumerate(((r.twk, r.kprev), (r.twv, r.vprev)))]

    k1_last, k1_before = [], []
    for d, to in enumerate(ps):
        for k, src in enumerate((r.twk, r.twv)):
            k1_last.append(send(src.at[pl.ds(0, 3), q16(to), :], r.ksl.at[k, pl.ds(4, 3)], r.k1_s.at[d, k], r.k1_r.at[k], in_plane(to)))
            k1_before.append(send(src.at[:, q16(to), :], r.ksl.at[k, pl.ds(0, 4)], r.k1_s.at[d, k], r.k1_r.at[2 + k], in_plane(to)))

    @pl.when(last)
    def _():
        start(k1_last)

    @pl.when(before)
    def _():
        start(k1_before)

    start(forks)

    @pl.when(has_next)
    def _():
        nb[0].start()
        nb[1].start()

    loads["tk"].wait()
    split_heads(r.v_tk, r.tmp, r.kh, TB, HD)
    loads["tv"].wait()
    split_heads(r.v_tv, r.tmp, r.vh, TB, HD)
    block_states(r.kh, r.vh, r.states)
    local_states(coef, r.states, r.local, r.local_bf, r.total)

    pa = [send(r.total.at[q64(to), :], r.xin.at[p], r.pa_s.at[d], r.pa_r.at[d], in_plane(to)) for d, to in enumerate(ps)]
    start(pa)
    r.xin[p] = r.total[q64(p), :]
    l1 = [send(r.local_bf.at[:, q64(to), :], r.lsl, r.l1_s.at[d], r.l1_r, in_plane(to)) for d, to in enumerate(ps)]

    @pl.when(last)
    def _():
        start(l1)
        r.lsl[...] = r.local_bf[:, q64(p), :]

    k3 = [send(r.ksl, r.ksl, r.k3_s.at[d], r.k3_r, in_column(to)) for d, to in enumerate(zs)]
    l3 = [send(r.lsl, r.lsl, r.l3_s.at[d], r.l3_r, in_column(to)) for d, to in enumerate(zs)]
    pz = [send(r.zin.at[z], r.zin.at[z], r.z_s.at[d], r.z_r.at[d], in_column(to)) for d, to in enumerate(zs)]
    ez = [send(r.ezin, r.ezin, r.ez_s.at[d], r.ez_r, in_column(to)) for d, to in enumerate(zs)]
    loads["twk"].wait()
    loads["twv"].wait()

    def context_to_planes():
        @pl.when(last_plane)
        def _():
            @pl.when(last)
            def _():
                for k, src in enumerate((r.v_twk, r.v_twv)):
                    r.ksl[k, 4:7] = src[0:3, q16(p), :]

            @pl.when(before)
            def _():
                for k, src in enumerate((r.v_twk, r.v_twv)):
                    r.ksl[k, 0:4] = src[:, q16(p), :]

            @pl.when(jnp.logical_not(last))
            def _():
                wait_recv(k1_last[:2])

            @pl.when(jnp.logical_not(before))
            def _():
                wait_recv(k1_before[:2])

            start(k3)

    hp = p // 2

    def plane_parts():
        parts = [r.xin[v].astype(F32) for v in range(NP)]
        return prefix16(parts, [coef(hp, level) for level in range(3, 7)])

    def prefix_plane():
        wait_recv(pa)
        total, prefix = plane_parts()
        r.zin[z] = total.astype(BF16)
        start(pz)

        @pl.when(last_plane)
        def _():
            r.ezin[...] = prefix(NP - 1).astype(BF16)
            start(ez)

    def local_to_planes():
        @pl.when(last_plane)
        def _():
            @pl.when(jnp.logical_not(last))
            def _():
                l1[0].wait_recv()

            start(l3)

    k5 = [send(r.kout.at[to], r.kctx.at[:, :, q16(p), :], r.k5_s.at[d], r.k5_r.at[d], in_plane(to)) for d, to in enumerate(ps)]

    def fork_of(v):
        return r.fk[v, 0:1, :]

    def context_back():
        @pl.when(jnp.logical_not(last_plane))
        def _():
            k3[0].wait_recv()

        wait_recv(forks)
        r.fk[p] = r.fk[NP]
        for k in range(2):
            for j in range(TB):
                blocks = [r.ksl[k, j + f].astype(F32) for f in range(TB)]
                for v in range(NP):
                    r.kout[v, k, j] = pick(fork_of(v), blocks).astype(BF16)
        start(k5)
        r.kctx[:, :, q16(p), :] = r.kout[p]

    xr = [send(r.rsend.at[to], r.cross.at[q64(p), :], r.xr_s.at[d], r.xr_r.at[d], in_plane(to)) for d, to in enumerate(ps)]
    xe = [send(r.esend.at[to], r.end.at[q64(p), :], r.xe_s.at[d], r.xe_r.at[d], in_plane(to)) for d, to in enumerate(ps)]

    def prefix_back():
        @pl.when(jnp.logical_not(last_plane))
        def _():
            ez[0].wait_recv()

        wait_recv(pz)
        zp = [r.zin[v].astype(F32) for v in range(NZ)]
        c7, c8, c9 = coef(hp, 7), coef(hp, 8), coef(hp, 9)
        z0, z1, z2 = z & 1, (z >> 1) & 1, (z >> 2) & 1
        half = (zp[0] + zp[1]) + (zp[2] + zp[3])
        low_pair, high_pair = zp[0] + zp[1], zp[4] + zp[5]
        cz = jnp.where(z2 == 1, c9 * half, 0.0)
        cz = cz + jnp.where(z1 == 1, c8 * jnp.where(z2 == 0, low_pair, high_pair), 0.0)
        cz = cz + jnp.where(z0 == 1, c7 * r.zin[z & 6].astype(F32), 0.0)
        r.ecross[...] = r.ezin[...].astype(F32) + (c9 * half + c8 * high_pair + c7 * zp[6])
        _, prefix = plane_parts()
        for v in range(NP):
            own = prefix(v)
            r.rsend[v] = (cz if own is None else cz + own).astype(BF16)
        start(xr)
        r.cross[q64(p), :] = r.rsend[p]

    def ends_back():
        @pl.when(jnp.logical_not(last_plane))
        def _():
            l3[0].wait_recv()

        base = r.ecross[...]
        ends = [base] + [base + r.lsl[f].astype(F32) for f in range(3)]
        for v in range(NP):
            r.esend[v] = pick(fork_of(v), ends).astype(BF16)
        start(xe)
        r.end[q64(p), :] = r.esend[p]

    bad = jnp.where(s == 0, TB, 0)
    tqr = r.wqh.at[:, pl.ds(0, TB * BLK), :]
    bqr = r.wqh.at[:, pl.ds(TB * BLK, BB * BLK), :]

    def branch_window(first, end):
        @pl.loop(first, end)
        def _(i):
            for g in range(KV):
                window_block(i, g, bqr, r.kb, r.vb, r.out, None, TB * BLK)

    def trunk_window(first, end):
        @pl.loop(first, end)
        def _(i):
            for g in range(KV):
                window_block(i, g, tqr, r.kt, r.vt, r.out, bad, 0)

    loads["bwk"].wait()
    loads["bwv"].wait()
    split_heads(r.v_bwk, r.tmp, r.kb, BB, KV, TB * BLK)
    split_heads(r.v_bwv, r.tmp, r.vb, BB, KV, TB * BLK)
    loads["bwq"].wait()
    split_heads(r.v_bwq, r.tmp, r.wqh, BB, HD, TB * BLK)
    context_to_planes()
    branch_window(4, 6)
    prefix_plane()

    branch_window(6, 7)
    local_to_planes()
    branch_window(7, 8)
    context_back()
    loads["twq"].wait()
    split_heads(r.v_twq, r.tmp, r.wqh, TB, HD)

    @pl.when(has_prev)
    def _():
        wait_recv(nb)

    @pl.when(jnp.logical_not(has_prev))
    def _():
        r.kprev[...] = jnp.zeros_like(r.kprev)
        r.vprev[...] = jnp.zeros_like(r.vprev)

    flat = lambda ref: ref.reshape(4 * 256, DH)
    split_heads(flat(r.kprev), r.tmp, r.kt, TB, KV)
    split_heads(flat(r.vprev), r.tmp, r.vt, TB, KV)
    split_heads(flat(r.v_twk), r.tmp, r.kt, TB, KV, TB * BLK)
    split_heads(flat(r.v_twv), r.tmp, r.vt, TB, KV, TB * BLK)
    trunk_window(0, 1)
    prefix_back()
    trunk_window(1, 4)
    ends_back()
    loads["tq"].wait()
    split_heads(r.v_tq, r.tmp, r.qh, TB, HD)
    loads["bq"].wait()
    split_heads(r.v_bq, r.tmp, r.bqh, BB, HD)
    wait_recv(k5)
    split_heads(flat(r.kctx.at[0]), r.tmp, r.kb, TB, KV)
    split_heads(flat(r.kctx.at[1]), r.tmp, r.vb, TB, KV)
    branch_window(0, 2)
    wait_recv(xr)

    @pl.loop(0, TB)
    def _(b):
        trunk_linear_block(b, coef, r.qh, r.kh, r.vh, r.local, r.cross, r.out)

    other = (s, 1 - head)
    sst = send(r.ss_t, r.ss_to, r.ss_s.at[0], r.ss_r.at[0], other)
    ssb = send(r.ss_b, r.ss_bo, r.ss_s.at[1], r.ss_r.at[1], other)
    trunk_out = r.out.at[:, pl.ds(0, TB * BLK), :]
    branch_out = r.out.at[:, pl.ds(TB * BLK, BB * BLK), :]

    @pl.loop(0, TB)
    def _(c):
        square_sums(trunk_out, c, r.ss_t)

    sst.start()
    branch_window(2, 4)
    wait_recv(xe)
    branch_linear(r.bqh, r.end, r.out)

    @pl.loop(0, BB)
    def _(c):
        square_sums(branch_out, c, r.ss_b)

    ssb.start()
    size = BLK * HD

    def write(buf, hbm, c, sem):
        return pltpu.make_async_copy(buf.at[rows_of(c * size, size), :], hbm.at[rows_of(c * size, size), :], sem)

    sst.wait()

    @pl.loop(0, TB)
    def _(c):
        scale_chunk(c, trunk_out, r.ss_t, r.ss_to, r.tmp, r.obuf_t)
        write(r.obuf_t, r.trunk_hbm, c, r.out_sem.at[c]).start()

    ssb.wait()

    @pl.loop(0, BB)
    def _(c):
        scale_chunk(c, branch_out, r.ss_b, r.ss_bo, r.tmp, r.obuf_b)
        write(r.obuf_b, r.branch_hbm, c, r.out_sem.at[TB + c]).start()

    wait_send(forks + pa + pz + k5 + xr + xe)

    @pl.when(has_next)
    def _():
        wait_send(nb)

    @pl.when(last)
    def _():
        wait_send(k1_last + l1)

    @pl.when(before)
    def _():
        wait_send(k1_before)

    @pl.when(last_plane)
    def _():
        wait_send(ez + k3 + l3)

    @pl.loop(0, TB)
    def _(c):
        write(r.obuf_t, r.trunk_hbm, c, r.out_sem.at[c]).wait()

    @pl.loop(0, BB)
    def _(c):
        write(r.obuf_b, r.branch_hbm, c, r.out_sem.at[TB + c]).wait()


SM = pl.BlockSpec(memory_space=pltpu.SMEM)
HBM = pl.BlockSpec(memory_space=pl.ANY)
VM = pl.BlockSpec(memory_space=pltpu.VMEM)
VMEM_LIMIT = 62 * 1024 * 1024
R = HD * DH
T = (TB + BB) * BLK


def sds(shape, dtype):
    return jax.ShapeDtypeStruct(shape, dtype)


def scratch_list():
    V, D = pltpu.VMEM, pltpu.SemaphoreType.DMA
    big = lambda rows: V((rows, DH), BF16)
    return dict(
        v_tk=big(4096), v_tv=big(4096), v_twk=V((4, 256, DH), BF16), v_twv=V((4, 256, DH), BF16),
        v_bwk=big(2048), v_bwv=big(2048), v_bwq=big(8192), v_twq=big(4096), v_tq=big(4096), v_bq=big(8192),
        load_sem=D((len(INPUTS),)), out_sem=D((TB + BB,)),
        tmp=V((BLK * HD, DH), F32), kh=V((HD, TB * BLK, DH), BF16), vh=V((HD, TB * BLK, DH), BF16),
        qh=V((HD, TB * BLK, DH), BF16), wqh=V((HD, T, DH), BF16), bqh=V((HD, BB * BLK, DH), BF16),
        kt=V((KV, 2 * TB * BLK, DH), BF16), vt=V((KV, 2 * TB * BLK, DH), BF16),
        kb=V((KV, T, DH), BF16), vb=V((KV, T, DH), BF16),
        out=V((HD, T, DH), F32), obuf_t=big(4096), obuf_b=big(8192),
        states=V((TB, R, DH), F32), local=V((3, R, DH), F32), local_bf=V((3, R, DH), BF16), total=V((R, DH), BF16),
        fk=V((NP + 1, 8, DH), F32), kprev=V((4, 256, DH), BF16), vprev=V((4, 256, DH), BF16),
        ksl=V((2, 7, 16, DH), BF16), kout=V((NP, 2, 4, 16, DH), BF16), kctx=V((2, 4, 256, DH), BF16),
        lsl=V((3, 64, DH), BF16), xin=V((NP, 64, DH), BF16), zin=V((NZ, 64, DH), BF16), ezin=V((64, DH), BF16),
        ecross=V((64, DH), F32), rsend=V((NP, 64, DH), BF16), esend=V((NP, 64, DH), BF16),
        cross=V((R, DH), BF16), end=V((R, DH), BF16),
        ss_t=V((8, DH), F32), ss_b=V((8, DH), F32), ss_to=V((8, DH), F32), ss_bo=V((8, DH), F32),
        fk_s=D((15,)), fk_r=D((15,)), nb_s=D((2,)), nb_r=D((2,)), k1_s=D((15, 2)), k1_r=D((4,)),
        pa_s=D((15,)), pa_r=D((15,)), l1_s=D((15,)), l1_r=D, z_s=D((7,)), z_r=D((7,)), ez_s=D((7,)), ez_r=D,
        k3_s=D((7,)), k3_r=D, l3_s=D((7,)), l3_r=D, k5_s=D((15,)), k5_r=D((15,)),
        xr_s=D((15,)), xr_r=D((15,)), xe_s=D((15,)), xe_r=D((15,)), ss_s=D((2,)), ss_r=D((2,)))


def shards(tq, tk, tv, twq, twk, twv, bq, bwq, bwk, bwv, gain, fork):
    flat = lambda a: a.reshape(-1, DH)
    blocks = lambda a: a.reshape(TB, KV * BLK, DH)
    scratch = scratch_list()
    names = ("gain", "fork") + INPUTS + ("trunk_hbm", "branch_hbm") + tuple(scratch)
    trunk_out, branch_out = pl.pallas_call(
        functools.partial(fused_kernel, names), name="fused",
        out_shape=(sds((TB * BLK * HD, DH), BF16), sds((BB * BLK * HD, DH), BF16)),
        in_specs=[SM, SM] + [HBM] * len(INPUTS), out_specs=(HBM, HBM),
        scratch_shapes=list(scratch.values()),
        compiler_params=pltpu.CompilerParams(vmem_limit_bytes=VMEM_LIMIT, collective_id=0, has_side_effects=True),
    )(gain, fork, flat(tk), flat(tv), blocks(twk), blocks(twv), flat(bwk), flat(bwv), flat(bwq), flat(twq), flat(tq), flat(bq))
    return trunk_out.reshape(TB * BLK, HD, DH), branch_out.reshape(BB * BLK, HD, DH)


def solution(mesh):
    spec = P("seq", "head", None)
    return jax.shard_map(
        shards, mesh=mesh, in_specs=(spec,) * 10 + (P("head", None), P("seq")),
        out_specs=(spec, spec), check_vma=False)
```
